32 devices in a mesh: rows: 16 (over z, x, core), cols: 2 (over y).
Axes of the slice: x: 2, y: 2, z: 4, core: 2. Of those that a mesh axis runs over, the one named last changes fastest.
Arguments:
- states: float32 [32, 16384], P('cols', 'rows'), may hold values from -120 to 120, as said below
- adj_weight: bfloat16 [128, 3, 128, 128], P('rows'), may hold values from 0.099609375 to 2
- adj_index: int32 [128, 3], P('rows'), may hold values from 0 to 127, as said below
- partner: int32 [128], P('rows'), may hold values from 0 to 127, as said below
Outputs:
- correction: float32 [32, 16384], P('cols', 'rows')
The draws below stay inside these ranges and needn't reach their ends.
Inputs may be any that keep to these rules, and one draw needn't show every extreme that they name: adj_index[b, 0] = b; every other entry lies within 4 blocks of b. partner[partner[b]] = b and partner[b] != b; the 8 blocks of one index of rows have their partners on 8 different other indices of rows, at most one block on each. `states`: finite values.
All inputs are finite; a program needn't handle non-finite values.
Results may differ from the reference program's by a relative error of at most 0.0003.
Values sent between devices are 32-bit elements; how exact they have to be, the bound alone decides.
No kernel may reach another device: no remote copies, remote signals or barrier semaphores. Data moves between devices by JAX's collectives and lax.ppermute only.
A program may use at most 64 MiB of HBM per device.

```python
import math
import jax
import jax.numpy as jnp
from jax import lax

BLK = 128
COLS = 32
NNZB = 3
BLK_DEV = 8
HB = 4
BLOCKS = 128
VERTS = 16384


def draw_states(key, part):
    key_rough, key_shared, key_mix = jax.random.split(key, 3)
    place = jnp.arange(VERTS, dtype=jnp.float32) / (VERTS - 1)
    rough = jax.random.normal(key_rough, (COLS, VERTS), jnp.float32)
    shared = jax.random.normal(key_shared, (VERTS,), jnp.float32)
    mixing = jax.random.uniform(key_mix, (COLS, 1), jnp.float32, 0.3, 1.0)
    scale = jnp.exp(jnp.log(10.0) * place)
    return jnp.clip(scale * (rough + mixing * shared), -110.0, 110.0)


def draw_adj_index(key, part):
    key_reach, key_sign = jax.random.split(key)
    blocks_all = jnp.arange(BLOCKS, dtype=jnp.int32)
    reach = jax.random.randint(key_reach, (BLOCKS, NNZB - 1), 1, HB + 1)
    signs = 2 * jax.random.randint(key_sign, (BLOCKS, NNZB - 1), 0, 2) - 1
    offsets = reach * signs
    position = blocks_all % BLK_DEV
    offsets = offsets.at[:, 0].set(jnp.where(position == 0, -HB, offsets[:, 0]))
    offsets = offsets.at[:, NNZB - 2].set(jnp.where(position == BLK_DEV - 1, HB, offsets[:, NNZB - 2]))
    target = blocks_all[:, None] + offsets
    outside = (target < 0) | (target >= BLOCKS)
    target = jnp.where(outside, blocks_all[:, None] - offsets, target)
    return jnp.concatenate([blocks_all[:, None], target], axis=1).astype(jnp.int32)


def draw_partner(key, part):
    row_devices = BLOCKS // BLK_DEV
    key_masks, key_orders = jax.random.split(key)
    masks = jax.random.permutation(key_masks, row_devices - 1)[:BLK_DEV].astype(jnp.int32) + 1
    orders = jax.vmap(lambda single: jax.random.permutation(single, BLK_DEV))(jax.random.split(key_orders, row_devices)).astype(jnp.int32)
    rounds = jnp.argsort(orders, axis=1).astype(jnp.int32)
    owners = jnp.arange(row_devices, dtype=jnp.int32)[:, None]
    other = jnp.bitwise_xor(owners, masks[rounds])
    partner_local = orders[other, rounds]
    return (other * BLK_DEV + partner_local).reshape(BLOCKS).astype(jnp.int32)


def level_of(key, dims, cuts, smallest, top_value):
    loudness, own = 1.0, jax.random.fold_in(key, 6)
    for dim, parts in cuts:
        heights = jnp.exp(jax.random.uniform(jax.random.fold_in(own, dim), (parts,), jnp.float32, smallest / len(cuts), top_value / len(cuts)))
        loudness = loudness * jnp.repeat(heights, dims[dim] // parts).reshape([-1 if axis == dim else 1 for axis in range(len(dims))])
    return loudness


def setup_inputs(seed: int = 0) -> dict:
    seeds = jax.random.split(jax.random.key(seed), 5)
    states = draw_states(jax.random.fold_in(seeds[4], 71), 0)
    adj_weight = jnp.clip(jnp.exp(math.log(2.0) - 2.9996462 * jax.random.uniform(seeds[1], (BLOCKS, NNZB, BLK, BLK), jnp.float32) ** level_of(seeds[1], (BLOCKS, NNZB, BLK, BLK), ((0, 16),), -0.2, 0.2)), 0.099609375, 2.0).astype(jnp.bfloat16)
    adj_index = draw_adj_index(jax.random.fold_in(seeds[4], 71), 0)
    partner = draw_partner(jax.random.fold_in(seeds[4], 71), 0)
    return dict(states=states, adj_weight=adj_weight, adj_index=adj_index, partner=partner)


DAMPING = 2.0 / 3.0
EPSILON = 1e-06
EXACT = lax.Precision.HIGHEST

def operate(vector_in, adj_weight, adj_index, degree):
    local_cols = vector_in.shape[0]
    grid_blocks = vector_in.reshape(local_cols, BLOCKS, BLK)

    def group_product(pieces):
        weight_group, index_group = pieces
        picked = grid_blocks[:, index_group]
        return jnp.einsum('gkij,cgkj->cgi', weight_group.astype(jnp.float32), picked.astype(jnp.float32), precision=EXACT, preferred_element_type=jnp.float32)
    grouped = lax.map(group_product, (adj_weight.reshape(BLOCKS // BLK_DEV, BLK_DEV, NNZB, BLK, BLK), adj_index.reshape(BLOCKS // BLK_DEV, BLK_DEV, NNZB)))
    neighbour = jnp.moveaxis(grouped, 0, 1).reshape(local_cols, VERTS)
    return degree * vector_in - neighbour

def pair_sum(values, partner):
    rows_here = values.shape[0]
    grid_blocks = values.reshape(rows_here, BLOCKS, BLK)
    return values + grid_blocks[:, partner].reshape(rows_here, VERTS)

def reference(states, adj_weight, adj_index, partner):
    degree = lax.optimization_barrier(jnp.sum(adj_weight, axis=(1, 3), dtype=jnp.float32)).reshape(VERTS)
    applied = operate(states, adj_weight, adj_index, degree)
    gram_matrix = jnp.einsum('cv,dv->cd', states * degree, states, precision=EXACT)
    rayleigh = jnp.einsum('cv,dv->cd', states, applied, precision=EXACT)
    factor = jnp.linalg.cholesky(gram_matrix)
    ritz_matrix = jax.scipy.linalg.cho_solve((factor, True), rayleigh)
    residual = applied - degree * jnp.einsum('cd,cv->dv', ritz_matrix, states, precision=EXACT)
    presmooth = DAMPING * residual / degree
    remain = residual - operate(presmooth, adj_weight, adj_index, degree)
    coarse = pair_sum(remain, partner)
    coarse_degree = pair_sum(degree[None, :], partner)[0]
    coarse_fix = DAMPING * coarse / coarse_degree
    coarse_image = pair_sum(operate(coarse_fix, adj_weight, adj_index, degree), partner)
    coarse_fix = coarse_fix + DAMPING * (coarse - coarse_image) / coarse_degree
    second = presmooth + coarse_fix
    smooth = second + DAMPING * (residual - operate(second, adj_weight, adj_index, degree)) / degree
    squares = lax.optimization_barrier(jnp.sum(smooth * smooth, axis=1))
    return smooth / jnp.sqrt(squares / VERTS + EPSILON)[:, None]
```

```python
import jax
import jax.numpy as jnp
from jax import lax
from jax.sharding import PartitionSpec as P

DAMPING = 2.0 / 3.0
EPSILON = 1e-06
EXACT = lax.Precision.HIGHEST


def extended(shard, sides, width):
    for axis, dim in sides:
        peers, length = (lax.axis_size(axis), shard.shape[dim])
        up = [(i, (i + 1) % peers) for i in range(peers - 1)]
        down = [(j, i) for i, j in up]
        last = lax.slice_in_dim(shard, length - width, length, axis=dim)
        initial = lax.slice_in_dim(shard, 0, width, axis=dim)
        before = lax.ppermute(last, axis, up)
        after = lax.ppermute(initial, axis, down)
        shard = jnp.concatenate([before, shard, after], axis=dim)
    return shard


def to_slots(values, owner_dev, row_devices):
    empty = jnp.zeros((values.shape[0], row_devices, values.shape[2]), values.dtype)
    return empty.at[:, owner_dev].set(values)


def from_slots(arrived, owner_dev):
    return arrived[:, owner_dev]


def summed(value, axis):
    peers, stride = (lax.axis_size(axis), 1)
    while stride < peers:
        left = peers // stride
        radix = 4 if left % 4 == 0 else (2 if left % 2 == 0 else left)
        total = value
        for step in range(1, radix):
            pairs = []
            for i in range(peers):
                digit = (i // stride) % radix
                pairs.append((i, i + ((digit + step) % radix - digit) * stride))
            if radix in (2, 4):
                pairs = [(i, i ^ (step * stride)) for i in range(peers)]
            total = total + lax.ppermute(value, axis, pairs)
        value = total
        stride *= radix
    return value


def solve_ritz(gram_matrix, rayleigh):
    factor = jnp.linalg.cholesky(gram_matrix)
    return jax.scipy.linalg.cho_solve((factor, True), rayleigh)


def local(states, adj_weight, adj_index, partner):
    local_cols, vertices = states.shape
    blocks_here = adj_weight.shape[0]
    block_len = adj_weight.shape[2]
    row_devices = lax.axis_size("rows")
    margin_blocks = blocks_here // 2
    local_ids = adj_index - (lax.axis_index("rows") * blocks_here - margin_blocks)
    owner_dev = partner // blocks_here
    degree = jnp.sum(adj_weight, axis=(1, 3), dtype=jnp.float32).reshape(vertices)
    degree_blocks = degree.reshape(1, blocks_here, block_len)

    def operate(vector_in):
        widened = extended(vector_in, (("rows", 1),), margin_blocks * block_len)
        grid_blocks = widened.reshape(local_cols, -1, block_len)
        picked = grid_blocks[:, local_ids]
        neighbour = jnp.einsum(
            "bkij,cbkj->cbi",
            adj_weight,
            picked,
            precision=EXACT,
            preferred_element_type=jnp.float32,
        )
        return degree * vector_in - neighbour.reshape(local_cols, vertices)

    applied = operate(states)
    all_states = lax.all_gather(states, "cols", axis=0, tiled=True)
    gram_part = jnp.einsum("cv,dv->cd", all_states * degree, all_states, precision=EXACT)
    rayleigh_part = jnp.einsum("cv,dv->cd", all_states, applied, precision=EXACT)
    both = summed(jnp.concatenate([gram_part, rayleigh_part], axis=1), "rows")
    columns = gram_part.shape[1]
    gram_matrix, rayleigh = both[:, :columns], both[:, columns:]
    ritz_matrix = solve_ritz(gram_matrix, rayleigh)
    residual = applied - degree * jnp.einsum("cd,cv->dv", ritz_matrix, all_states, precision=EXACT)
    presmooth = DAMPING * residual / degree
    remain = (residual - operate(presmooth)).reshape(local_cols, blocks_here, block_len)
    arrived, arrived_degree = (
        lax.all_to_all(
            to_slots(remain, owner_dev, row_devices),
            "rows",
            split_axis=1,
            concat_axis=1,
            tiled=True,
        ),
        lax.all_to_all(
            to_slots(degree_blocks, owner_dev, row_devices),
            "rows",
            split_axis=1,
            concat_axis=1,
            tiled=True,
        ),
    )
    coarse_degree = (degree_blocks + from_slots(arrived_degree, owner_dev)).reshape(vertices)
    coarse = (remain + from_slots(arrived, owner_dev)).reshape(local_cols, vertices)
    coarse_fix = DAMPING * coarse / coarse_degree
    product = operate(coarse_fix).reshape(local_cols, blocks_here, block_len)
    arrived_product = lax.all_to_all(
        to_slots(product, owner_dev, row_devices), "rows", split_axis=1, concat_axis=1, tiled=True
    )
    coarse_image = (product + from_slots(arrived_product, owner_dev)).reshape(local_cols, vertices)
    coarse_fix = coarse_fix + DAMPING * (coarse - coarse_image) / coarse_degree
    second = presmooth + coarse_fix
    smooth = second + DAMPING * (residual - operate(second)) / degree
    squares = summed(jnp.sum(smooth * smooth, axis=1), "rows")
    return smooth / jnp.sqrt(squares / (vertices * row_devices) + EPSILON)[:, None]


def solution(mesh):
    return jax.shard_map(
        local,
        mesh=mesh,
        in_specs=(P("cols", "rows"), P("rows", None, None, None), P("rows", None), P("rows")),
        out_specs=P("cols", "rows"),
        check_vma=False,
    )
```

```python
import jax
import jax.numpy as jnp
from jax import lax
from jax.experimental import pallas as pl
from jax.experimental.pallas import tpu as pltpu
from jax.sharding import PartitionSpec as P

DAMPING = 2.0 / 3.0
KEEP = 1.0 - DAMPING
EPSILON = 1e-06
EXACT = lax.Precision.HIGHEST
PARTS = 3
F32 = jnp.float32
IN_VMEM = pl.BlockSpec(memory_space=pltpu.VMEM)
IN_SMEM = pl.BlockSpec(memory_space=pltpu.SMEM)


def kernel_call(body, name, outs, scalars, arrays, scratch=(), cost=2_000_000):
    return pl.pallas_call(
        body,
        name=name,
        out_shape=[jax.ShapeDtypeStruct(shape, F32) for shape in outs],
        in_specs=[IN_SMEM] * len(scalars) + [IN_VMEM] * len(arrays),
        out_specs=[IN_VMEM] * len(outs),
        scratch_shapes=list(scratch),
        cost_estimate=pl.CostEstimate(flops=cost, bytes_accessed=cost, transcendentals=0),
    )(*scalars, *arrays)


def radices(peers):
    found = []
    while peers > 1:
        found.append(4 if peers % 4 == 0 else 2)
        peers //= found[-1]
    return found


def exchanged(value, axis, stride, radix):
    peers = lax.axis_size(axis)
    return [value] + [
        lax.ppermute(value, axis, [(i, i ^ (mask * stride)) for i in range(peers)])
        for mask in range(1, radix)
    ]


def from_sides(last, first, axis):
    peers = lax.axis_size(axis)
    up = [(i, i + 1) for i in range(peers - 1)]
    return lax.ppermute(last, axis, up), lax.ppermute(first, axis, [(j, i) for i, j in up])


def each(count, body):
    if count <= 8:
        for step in range(count):
            body(step)
    else:
        lax.fori_loop(0, count, lambda step, carry: (body(step), carry)[1], 0)


def lanes(block, length):
    start = block * length
    return pl.ds(start if isinstance(block, int) else pl.multiple_of(start, length), length)


def padded(value, rows):
    if value.shape[0] == rows:
        return value
    return jnp.concatenate([value, jnp.zeros((rows - value.shape[0], value.shape[1]), F32)], axis=0)


def in_parts(value):
    pieces = []
    for _ in range(PARTS):
        piece = value.astype(jnp.bfloat16)
        pieces.append(piece)
        value = value - piece.astype(F32)
    return jnp.concatenate(pieces, axis=0)


def fill(field, base, value, length):
    split = in_parts(value)
    for block in range(value.shape[1] // length):
        field[base + block, : split.shape[0], :] = split[:, block * length : (block + 1) * length]


def fill_extended(field, before, own, after, length):
    count = before.shape[1] // length
    fill(field, 0, before, length)
    fill(field, count, own, length)
    fill(field, count + own.shape[1] // length, after, length)


def neighbours(index, weight, field, block):
    blocks = index.shape[0]
    shift = blocks // 2 - index[0, 0]
    total = None
    for k in range(index.shape[1]):
        term = lax.dot_general(
            field[index[block, k] + shift],
            weight[block, k],
            (((1,), (1,)), ((), ())),
            preferred_element_type=F32,
        )
        total = term if total is None else total + term
    return total


def folded(total, rows):
    return total[:rows] + total[rows : 2 * rows] + total[2 * rows : PARTS * rows]


def solved(matrix, size):
    row_id = lax.broadcasted_iota(jnp.int32, matrix.shape, 0)
    for k in range(0, size, 2):
        left = jnp.broadcast_to(matrix[:, k : k + 1], matrix.shape)
        right = jnp.broadcast_to(matrix[:, k + 1 : k + 2], matrix.shape)
        upper, lower = matrix[k : k + 1], matrix[k + 1 : k + 2]
        pivot, cross = left[k : k + 1], right[k : k + 1]
        ratio = left[k + 1 : k + 2] / pivot
        new_lower = (lower - ratio * upper) / (right[k + 1 : k + 2] - ratio * cross)
        new_upper = (upper - cross * new_lower) / pivot
        rest = matrix - left * new_upper - right * new_lower
        matrix = jnp.where(row_id == k, new_upper, jnp.where(row_id == k + 1, new_lower, rest))
    return matrix


def local(states, adj_weight, adj_index, partner):
    local_cols, vertices = states.shape
    blocks, _, length, _ = adj_weight.shape
    row_devices, col_devices = lax.axis_size("rows"), lax.axis_size("cols")
    total_cols = local_cols * col_devices
    width = (blocks // 2) * length
    rows = -(-local_cols // 16) * 16
    stages = radices(row_devices)
    field_shape = (2 * blocks, PARTS * rows, length)
    field = pltpu.VMEM(field_shape, jnp.bfloat16)
    full, edge, line = (rows, vertices), (rows, width), (1, vertices)
    slots = (row_devices, rows, length)

    def first_body(index, weight, before, after, *refs):
        peers, (payload, image, sent, scaled, last, first, degree, ones_field) = (
            refs[:col_devices],
            refs[col_devices:],
        )
        fill_extended(
            ones_field,
            padded(before[...], rows),
            padded(peers[0][...], rows),
            padded(after[...], rows),
            length,
        )
        ones_field[:, PARTS * rows :, :] = jnp.ones((2 * blocks, 16, length), jnp.bfloat16)
        payload[...] = jnp.zeros(payload.shape, F32)

        def one(block):
            total = neighbours(index, weight, ones_field, block)
            here = total[PARTS * rows : PARTS * rows + 1]
            value = folded(total, rows)
            at = lanes(block, length)
            degree[:, at] = here
            payload[pl.ds(total_cols + block, 1), :] = here
            image[:, at] = value
            scaled[:, at] = value / here

        each(blocks, one)
        everyone = jnp.concatenate([peer[...] for peer in peers], axis=0)
        other = jnp.concatenate([everyone * degree[...], image[...]], axis=0)
        payload[:total_cols, : total_cols + rows] = lax.dot_general(
            everyone, other, (((1,), (1,)), ((), ())), precision=EXACT, preferred_element_type=F32
        )
        sent[...] = image[:local_cols, :]
        last[...] = scaled[:, vertices - width :]
        first[...] = scaled[:, :width]

    def second_body(index, weight, before, after, scaled, image, offset, spread):
        fill_extended(spread, before[...], scaled[...], after[...], length)

        def one(block):
            at = lanes(block, length)
            value = folded(neighbours(index, weight, spread, block), rows)
            offset[:, at] = KEEP * image[:, at] + DAMPING * value

        each(blocks, one)

    def ritz_body(index, mates, *refs):
        pieces, refs = refs[: stages[-1]], refs[stages[-1] :]
        peers, refs = refs[:col_devices], refs[col_devices:]
        images, refs = refs[:col_devices], refs[col_devices:]
        own_image, scaled, offset, degree, out, remain, residual, presmooth, pair_degree, table = refs
        group = row_devices // stages[-1] * blocks
        total = pieces[0][:total_cols, :]
        for piece in pieces[1:]:
            total = total + piece[:total_cols, :]
        for place, piece in enumerate(pieces):
            table[place * group : (place + 1) * group, :] = piece[total_cols:, :]
        ritz = jnp.transpose(solved(total, total_cols))[total_cols : total_cols + rows]
        everyone = jnp.concatenate([peer[...] for peer in peers], axis=0)
        spread = jnp.concatenate([image[...] for image in images], axis=0)
        mixed = jnp.dot(ritz, everyone, precision=EXACT, preferred_element_type=F32)
        mixed_image = jnp.dot(ritz, spread, precision=EXACT, preferred_element_type=F32)
        weighted = degree[...] * mixed
        residual[...] = weighted - own_image[...]
        presmooth[...] = DAMPING * (mixed - scaled[...])
        remain[...] = KEEP * weighted + DAMPING * mixed_image - offset[...]
        me = lax.div(index[0, 0], blocks)

        def one(block):
            at = lanes(block, length)
            owner = lax.div(mates[block], blocks)
            row = lax.bitwise_xor(owner, me) * blocks + (mates[block] - owner * blocks)
            out[owner] = remain[:, at]
            pair_degree[:, at] = degree[:, at] + table[pl.ds(row, 1), :]

        each(blocks, one)

    def coarse_body(mates, arrived, remain, pair_degree, coarse, fix, last, first):
        def one(block):
            at = lanes(block, length)
            value = remain[:, at] + arrived[lax.div(mates[block], blocks)]
            coarse[:, at] = value
            fix[:, at] = DAMPING * value / pair_degree[:, at]

        each(blocks, one)
        last[...] = fix[:, vertices - width :]
        first[...] = fix[:, :width]

    def product_body(index, mates, weight, before, after, fix, degree, out, product, spread):
        fill_extended(spread, before[...], fix[...], after[...], length)

        def one(block):
            at = lanes(block, length)
            value = degree[:, at] * fix[:, at] - folded(neighbours(index, weight, spread, block), rows)
            product[:, at] = value
            out[lax.div(mates[block], blocks)] = value

        each(blocks, one)

    def fix_body(mates, arrived, product, coarse, fix, pair_degree, presmooth, second, last, first):
        def one(block):
            at = lanes(block, length)
            image = product[:, at] + arrived[lax.div(mates[block], blocks)]
            step = DAMPING * (coarse[:, at] - image) / pair_degree[:, at]
            second[:, at] = presmooth[:, at] + (fix[:, at] + step)

        each(blocks, one)
        last[...] = second[:, vertices - width :]
        first[...] = second[:, :width]

    def smooth_body(index, weight, before, after, second, residual, degree, smooth, squares, spread):
        fill_extended(spread, before[...], second[...], after[...], length)

        def one(block):
            at = lanes(block, length)
            value, here = second[:, at], degree[:, at]
            image = here * value - folded(neighbours(index, weight, spread, block), rows)
            smooth[:, at] = value + DAMPING * (residual[:, at] - image) / here

        each(blocks, one)
        value = smooth[...]
        squares[...] = jnp.broadcast_to(jnp.sum(value * value, axis=1, keepdims=True), squares.shape)

    def scale_body(*refs):
        smooth, correction = refs[-2:]
        total = refs[0][...]
        for piece in refs[1:-2]:
            total = total + piece[...]
        norm = jnp.sqrt(total[:local_cols, :1] / (vertices * row_devices) + EPSILON)
        correction[...] = smooth[:local_cols, :] / norm

    before, after = from_sides(states[:, vertices - width :], states[:, :width], "rows")
    peers = exchanged(states, "cols", 1, col_devices)
    payload, image, sent, scaled, last, first, degree = kernel_call(
        first_body,
        "image",
        [(total_cols + blocks, length), full, (local_cols, vertices), full, edge, edge, line],
        [adj_index],
        [adj_weight, before, after, *peers],
        [pltpu.VMEM((2 * blocks, PARTS * rows + 16, length), jnp.bfloat16)],
    )
    stride = 1
    for place, radix in enumerate(stages):
        pieces = exchanged(payload, "rows", stride, radix)
        stride *= radix
        if place + 1 < len(stages):
            summed = pieces[0][:total_cols]
            for piece in pieces[1:]:
                summed = summed + piece[:total_cols]
            payload = jnp.concatenate([summed] + [piece[total_cols:] for piece in pieces], axis=0)
    before, after = from_sides(last, first, "rows")
    images = exchanged(sent, "cols", 1, col_devices)
    (offset,) = kernel_call(
        second_body, "offset", [full], [adj_index], [adj_weight, before, after, scaled, image], [field]
    )
    out, remain, residual, presmooth, pair_degree = kernel_call(
        ritz_body,
        "ritz",
        [slots, full, full, full, line],
        [adj_index, partner],
        [*pieces, *peers, *images, image, scaled, offset, degree],
        [pltpu.VMEM((row_devices * blocks, length), F32)],
    )
    arrived = lax.all_to_all(out, "rows", split_axis=0, concat_axis=0, tiled=True)
    coarse, fix, last, first = kernel_call(
        coarse_body, "coarse", [full, full, edge, edge], [partner], [arrived, remain, pair_degree]
    )
    before, after = from_sides(last, first, "rows")
    out, product = kernel_call(
        product_body,
        "product",
        [slots, full],
        [adj_index, partner],
        [adj_weight, before, after, fix, degree],
        [field],
    )
    arrived = lax.all_to_all(out, "rows", split_axis=0, concat_axis=0, tiled=True)
    second, last, first = kernel_call(
        fix_body,
        "fix",
        [full, edge, edge],
        [partner],
        [arrived, product, coarse, fix, pair_degree, presmooth],
    )
    before, after = from_sides(last, first, "rows")
    smooth, squares = kernel_call(
        smooth_body,
        "smooth",
        [full, (rows, length)],
        [adj_index],
        [adj_weight, before, after, second, residual, degree],
        [field],
    )
    stride = 1
    for place, radix in enumerate(stages):
        pieces = exchanged(squares, "rows", stride, radix)
        stride *= radix
        if place + 1 < len(stages):
            squares = pieces[0]
            for piece in pieces[1:]:
                squares = squares + piece
    (correction,) = kernel_call(scale_body, "scale", [states.shape], [], [*pieces, smooth])
    return correction


def solution(mesh):
    return jax.shard_map(
        local,
        mesh=mesh,
        in_specs=(P("cols", "rows"), P("rows", None, None, None), P("rows", None), P("rows")),
        out_specs=P("cols", "rows"),
        check_vma=False,
    )
```

```python
import jax
import jax.numpy as jnp
from jax import lax
from jax.experimental import pallas as pl
from jax.experimental.pallas import tpu as pltpu
from jax.sharding import PartitionSpec as P

DAMPING = 2.0 / 3.0
KEEP = 1.0 - DAMPING
EPSILON = 1e-06
EXACT = lax.Precision.HIGHEST
PARTS = 3
VMEM_GRANT = 16 * 1024 * 1024
F32 = jnp.float32
IN_VMEM = pl.BlockSpec(memory_space=pltpu.VMEM)
IN_SMEM = pl.BlockSpec(memory_space=pltpu.SMEM)


def kernel_call(body, name, outs, scalars, arrays, scratch=(), cost=2_000_000):
    return pl.pallas_call(
        body,
        name=name,
        out_shape=[jax.ShapeDtypeStruct(shape, F32) for shape in outs],
        in_specs=[IN_SMEM] * len(scalars) + [IN_VMEM] * len(arrays),
        out_specs=[IN_VMEM] * len(outs),
        scratch_shapes=list(scratch),
        compiler_params=pltpu.CompilerParams(vmem_limit_bytes=VMEM_GRANT),
        cost_estimate=pl.CostEstimate(flops=cost, bytes_accessed=cost, transcendentals=0),
    )(*scalars, *arrays)


def radices(peers):
    found = []
    while peers > 1:
        found.append(4 if peers % 4 == 0 else 2)
        peers //= found[-1]
    return found


def exchanged(value, axis, stride, radix):
    peers = lax.axis_size(axis)
    return [value] + [
        lax.ppermute(value, axis, [(i, i ^ (mask * stride)) for i in range(peers)])
        for mask in range(1, radix)
    ]


def from_sides(last, first, axis):
    peers = lax.axis_size(axis)
    up = [(i, i + 1) for i in range(peers - 1)]
    return lax.ppermute(last, axis, up), lax.ppermute(first, axis, [(j, i) for i, j in up])


def each(count, body):
    if count <= 8:
        for step in range(count):
            body(step)
    else:
        lax.fori_loop(0, count, lambda step, carry: (body(step), carry)[1], 0)


def lanes(block, length):
    start = block * length
    return pl.ds(start if isinstance(block, int) else pl.multiple_of(start, length), length)


def padded(value, rows):
    if value.shape[0] == rows:
        return value
    return jnp.concatenate([value, jnp.zeros((rows - value.shape[0], value.shape[1]), F32)], axis=0)


def in_parts(value):
    pieces = []
    for _ in range(PARTS):
        piece = value.astype(jnp.bfloat16)
        pieces.append(piece)
        value = value - piece.astype(F32)
    return jnp.concatenate(pieces, axis=0)


def fill(field, base, value, length):
    split = in_parts(value)
    for block in range(value.shape[1] // length):
        field[base + block, : split.shape[0], :] = split[:, block * length : (block + 1) * length]


def fill_extended(field, before, own, after, length):
    count = before.shape[1] // length
    fill(field, 0, before, length)
    fill(field, count, own, length)
    fill(field, count + own.shape[1] // length, after, length)


def neighbours(index, weight, field, block):
    blocks = index.shape[0]
    shift = blocks // 2 - index[0, 0]
    total = None
    for k in range(index.shape[1]):
        term = lax.dot_general(
            field[index[block, k] + shift],
            weight[block, k],
            (((1,), (1,)), ((), ())),
            preferred_element_type=F32,
        )
        total = term if total is None else total + term
    return total


def folded(total, rows):
    return total[:rows] + total[rows : 2 * rows] + total[2 * rows : PARTS * rows]


def solved(matrix, size):
    row_id = lax.broadcasted_iota(jnp.int32, matrix.shape, 0)
    for k in range(0, size, 2):
        left = jnp.broadcast_to(matrix[:, k : k + 1], matrix.shape)
        right = jnp.broadcast_to(matrix[:, k + 1 : k + 2], matrix.shape)
        upper, lower = matrix[k : k + 1], matrix[k + 1 : k + 2]
        pivot, cross = left[k : k + 1], right[k : k + 1]
        ratio = left[k + 1 : k + 2] / pivot
        new_lower = (lower - ratio * upper) / (right[k + 1 : k + 2] - ratio * cross)
        new_upper = (upper - cross * new_lower) / pivot
        rest = matrix - left * new_upper - right * new_lower
        matrix = jnp.where(row_id == k, new_upper, jnp.where(row_id == k + 1, new_lower, rest))
    return matrix


def local(states, adj_weight, adj_index, partner):
    local_cols, vertices = states.shape
    blocks, _, length, _ = adj_weight.shape
    row_devices, col_devices = lax.axis_size("rows"), lax.axis_size("cols")
    total_cols = local_cols * col_devices
    width = (blocks // 2) * length
    rows = -(-local_cols // 16) * 16
    stages = radices(row_devices)
    field_shape = (2 * blocks, PARTS * rows, length)
    field = pltpu.VMEM(field_shape, jnp.bfloat16)
    full, edge, line = (rows, vertices), (rows, width), (1, vertices)
    slots = (row_devices, rows, length)

    def first_body(index, weight, before, after, *refs):
        peers, (payload, image, sent, scaled, last, first, degree, ones_field) = (
            refs[:col_devices],
            refs[col_devices:],
        )
        fill_extended(
            ones_field,
            padded(before[...], rows),
            padded(peers[0][...], rows),
            padded(after[...], rows),
            length,
        )
        ones_field[:, PARTS * rows :, :] = jnp.ones((2 * blocks, 16, length), jnp.bfloat16)
        payload[...] = jnp.zeros(payload.shape, F32)

        def one(block):
            total = neighbours(index, weight, ones_field, block)
            here = total[PARTS * rows : PARTS * rows + 1]
            value = folded(total, rows)
            at = lanes(block, length)
            degree[:, at] = here
            payload[pl.ds(total_cols + block, 1), :] = here
            image[:, at] = value
            scaled[:, at] = value / here

        each(blocks, one)
        everyone = jnp.concatenate([peer[...] for peer in peers], axis=0)
        other = jnp.concatenate([everyone * degree[...], image[...]], axis=0)
        payload[:total_cols, : total_cols + rows] = lax.dot_general(
            everyone, other, (((1,), (1,)), ((), ())), precision=EXACT, preferred_element_type=F32
        )
        sent[...] = image[:local_cols, :]
        last[...] = scaled[:, vertices - width :]
        first[...] = scaled[:, :width]

    def second_body(index, weight, before, after, scaled, image, offset, spread):
        fill_extended(spread, before[...], scaled[...], after[...], length)

        def one(block):
            at = lanes(block, length)
            value = folded(neighbours(index, weight, spread, block), rows)
            offset[:, at] = KEEP * image[:, at] + DAMPING * value

        each(blocks, one)

    def ritz_body(index, mates, *refs):
        pieces, refs = refs[: stages[-1]], refs[stages[-1] :]
        peers, refs = refs[:col_devices], refs[col_devices:]
        images, refs = refs[:col_devices], refs[col_devices:]
        own_image, scaled, offset, degree, out, remain, residual, presmooth, pair_degree, table = refs
        group = row_devices // stages[-1] * blocks
        total = pieces[0][:total_cols, :]
        for piece in pieces[1:]:
            total = total + piece[:total_cols, :]
        for place, piece in enumerate(pieces):
            table[place * group : (place + 1) * group, :] = piece[total_cols:, :]
        ritz = jnp.transpose(solved(total, total_cols))[total_cols : total_cols + rows]
        everyone = jnp.concatenate([peer[...] for peer in peers], axis=0)
        spread = jnp.concatenate([image[...] for image in images], axis=0)
        mixed = jnp.dot(ritz, everyone, precision=EXACT, preferred_element_type=F32)
        mixed_image = jnp.dot(ritz, spread, precision=EXACT, preferred_element_type=F32)
        weighted = degree[...] * mixed
        residual[...] = weighted - own_image[...]
        presmooth[...] = DAMPING * (mixed - scaled[...])
        remain[...] = KEEP * weighted + DAMPING * mixed_image - offset[...]
        me = lax.div(index[0, 0], blocks)

        def one(block):
            at = lanes(block, length)
            owner = lax.div(mates[block], blocks)
            row = lax.bitwise_xor(owner, me) * blocks + (mates[block] - owner * blocks)
            out[owner] = remain[:, at]
            pair_degree[:, at] = degree[:, at] + table[pl.ds(row, 1), :]

        each(blocks, one)

    def coarse_body(mates, arrived, remain, pair_degree, coarse, fix, last, first):
        def one(block):
            at = lanes(block, length)
            value = remain[:, at] + arrived[lax.div(mates[block], blocks)]
            coarse[:, at] = value
            fix[:, at] = DAMPING * value / pair_degree[:, at]

        each(blocks, one)
        last[...] = fix[:, vertices - width :]
        first[...] = fix[:, :width]

    def product_body(index, mates, weight, before, after, fix, degree, out, product, spread):
        fill_extended(spread, before[...], fix[...], after[...], length)

        def one(block):
            at = lanes(block, length)
            value = degree[:, at] * fix[:, at] - folded(neighbours(index, weight, spread, block), rows)
            product[:, at] = value
            out[lax.div(mates[block], blocks)] = value

        each(blocks, one)

    def fix_body(mates, arrived, product, coarse, fix, pair_degree, presmooth, second, last, first):
        def one(block):
            at = lanes(block, length)
            image = product[:, at] + arrived[lax.div(mates[block], blocks)]
            step = DAMPING * (coarse[:, at] - image) / pair_degree[:, at]
            second[:, at] = presmooth[:, at] + (fix[:, at] + step)

        each(blocks, one)
        last[...] = second[:, vertices - width :]
        first[...] = second[:, :width]

    def smooth_body(index, weight, before, after, second, residual, degree, smooth, squares, spread):
        fill_extended(spread, before[...], second[...], after[...], length)

        def one(block):
            at = lanes(block, length)
            value, here = second[:, at], degree[:, at]
            image = here * value - folded(neighbours(index, weight, spread, block), rows)
            smooth[:, at] = value + DAMPING * (residual[:, at] - image) / here

        each(blocks, one)
        value = smooth[...]
        squares[...] = jnp.broadcast_to(jnp.sum(value * value, axis=1, keepdims=True), squares.shape)

    def scale_body(*refs):
        smooth, correction = refs[-2:]
        total = refs[0][...]
        for piece in refs[1:-2]:
            total = total + piece[...]
        norm = jnp.sqrt(total[:local_cols, :1] / (vertices * row_devices) + EPSILON)
        correction[...] = smooth[:local_cols, :] / norm

    before, after = from_sides(states[:, vertices - width :], states[:, :width], "rows")
    peers = exchanged(states, "cols", 1, col_devices)
    payload, image, sent, scaled, last, first, degree = kernel_call(
        first_body,
        "image",
        [(total_cols + blocks, length), full, (local_cols, vertices), full, edge, edge, line],
        [adj_index],
        [adj_weight, before, after, *peers],
        [pltpu.VMEM((2 * blocks, PARTS * rows + 16, length), jnp.bfloat16)],
    )
    stride = 1
    for place, radix in enumerate(stages):
        pieces = exchanged(payload, "rows", stride, radix)
        stride *= radix
        if place + 1 < len(stages):
            summed = pieces[0][:total_cols]
            for piece in pieces[1:]:
                summed = summed + piece[:total_cols]
            payload = jnp.concatenate([summed] + [piece[total_cols:] for piece in pieces], axis=0)
    before, after = from_sides(last, first, "rows")
    images = exchanged(sent, "cols", 1, col_devices)
    (offset,) = kernel_call(
        second_body, "offset", [full], [adj_index], [adj_weight, before, after, scaled, image], [field]
    )
    out, remain, residual, presmooth, pair_degree = kernel_call(
        ritz_body,
        "ritz",
        [slots, full, full, full, line],
        [adj_index, partner],
        [*pieces, *peers, *images, image, scaled, offset, degree],
        [pltpu.VMEM((row_devices * blocks, length), F32)],
    )
    arrived = lax.all_to_all(out, "rows", split_axis=0, concat_axis=0, tiled=True)
    coarse, fix, last, first = kernel_call(
        coarse_body, "coarse", [full, full, edge, edge], [partner], [arrived, remain, pair_degree]
    )
    before, after = from_sides(last, first, "rows")
    out, product = kernel_call(
        product_body,
        "product",
        [slots, full],
        [adj_index, partner],
        [adj_weight, before, after, fix, degree],
        [field],
    )
    arrived = lax.all_to_all(out, "rows", split_axis=0, concat_axis=0, tiled=True)
    second, last, first = kernel_call(
        fix_body,
        "fix",
        [full, edge, edge],
        [partner],
        [arrived, product, coarse, fix, pair_degree, presmooth],
    )
    before, after = from_sides(last, first, "rows")
    smooth, squares = kernel_call(
        smooth_body,
        "smooth",
        [full, (rows, length)],
        [adj_index],
        [adj_weight, before, after, second, residual, degree],
        [field],
    )
    stride = 1
    for place, radix in enumerate(stages):
        pieces = exchanged(squares, "rows", stride, radix)
        stride *= radix
        if place + 1 < len(stages):
            squares = pieces[0]
            for piece in pieces[1:]:
                squares = squares + piece
    (correction,) = kernel_call(scale_body, "scale", [states.shape], [], [*pieces, smooth])
    return correction


def solution(mesh):
    return jax.shard_map(
        local,
        mesh=mesh,
        in_specs=(P("cols", "rows"), P("rows", None, None, None), P("rows", None), P("rows")),
        out_specs=P("cols", "rows"),
        check_vma=False,
    )
```

```python
import jax
import jax.numpy as jnp
from jax import lax
from jax.experimental import pallas as pl
from jax.experimental.pallas import tpu as pltpu
from jax.sharding import PartitionSpec as P

DAMPING = 2.0 / 3.0
KEEP = 1.0 - DAMPING
EPSILON = 1e-06
EXACT = lax.Precision.HIGHEST
PARTS = 3
VMEM_GRANT = 16 * 1024 * 1024
F32 = jnp.float32
IN_VMEM = pl.BlockSpec(memory_space=pltpu.VMEM)
IN_SMEM = pl.BlockSpec(memory_space=pltpu.SMEM)


def kernel_call(body, name, outs, scalars, arrays, scratch=(), cost=2_000_000):
    return pl.pallas_call(
        body,
        name=name,
        out_shape=[jax.ShapeDtypeStruct(shape, F32) for shape in outs],
        in_specs=[IN_SMEM] * len(scalars) + [IN_VMEM] * len(arrays),
        out_specs=[IN_VMEM] * len(outs),
        scratch_shapes=list(scratch),
        compiler_params=pltpu.CompilerParams(vmem_limit_bytes=VMEM_GRANT),
        cost_estimate=pl.CostEstimate(flops=cost, bytes_accessed=cost, transcendentals=0),
    )(*scalars, *arrays)


def radices(peers):
    found = []
    while peers > 1:
        found.append(4 if peers % 4 == 0 else 2)
        peers //= found[-1]
    return found


def exchanged(value, axis, stride, radix):
    peers = lax.axis_size(axis)
    return [value] + [
        lax.ppermute(value, axis, [(i, i ^ (mask * stride)) for i in range(peers)])
        for mask in range(1, radix)
    ]


def from_pairs(inner, outer, axis):
    peers = lax.axis_size(axis)
    up = [(i, i + 1) for i in range(1, peers - 1, 2)]
    return (
        lax.ppermute(outer, axis, up + [(j, i) for i, j in up]),
        lax.ppermute(inner, axis, [(i, i ^ 1) for i in range(peers)]),
    )


def each(count, body):
    if count <= 8:
        for step in range(count):
            body(step)
    else:
        lax.fori_loop(0, count, lambda step, carry: (body(step), carry)[1], 0)


def lanes(block, length):
    start = block * length
    return pl.ds(start if isinstance(block, int) else pl.multiple_of(start, length), length)


def padded(value, rows):
    if value.shape[0] == rows:
        return value
    return jnp.concatenate([value, jnp.zeros((rows - value.shape[0], value.shape[1]), F32)], axis=0)


def in_parts(value):
    pieces = []
    for _ in range(PARTS):
        piece = value.astype(jnp.bfloat16)
        pieces.append(piece)
        value = value - piece.astype(F32)
    return jnp.concatenate(pieces, axis=0)


def fill(field, base, value, length):
    split = in_parts(value)
    for block in range(value.shape[1] // length):
        field[base + block, : split.shape[0], :] = split[:, block * length : (block + 1) * length]


def parity_of(index):
    return lax.rem(lax.div(index[0, 0], index.shape[0]), 2)


def half(parity, vertices, width, length):
    return pl.ds(pl.multiple_of(parity * (vertices - width), length), width)


def fill_extended(field, parity, outer, own, inner, length):
    margin, blocks = outer.shape[1] // length, own.shape[1] // length
    fill(field, parity * (margin + blocks), outer, length)
    fill(field, margin, own, length)
    fill(field, (1 - parity) * (margin + blocks), inner, length)


def neighbours(index, weight, field, block):
    blocks = index.shape[0]
    shift = blocks // 2 - index[0, 0]
    total = None
    for k in range(index.shape[1]):
        term = lax.dot_general(
            field[index[block, k] + shift],
            weight[block, k],
            (((1,), (1,)), ((), ())),
            preferred_element_type=F32,
        )
        total = term if total is None else total + term
    return total


def folded(total, rows):
    return total[:rows] + total[rows : 2 * rows] + total[2 * rows : PARTS * rows]


def solved(matrix, size):
    row_id = lax.broadcasted_iota(jnp.int32, matrix.shape, 0)
    for k in range(0, size, 2):
        left = jnp.broadcast_to(matrix[:, k : k + 1], matrix.shape)
        right = jnp.broadcast_to(matrix[:, k + 1 : k + 2], matrix.shape)
        upper, lower = matrix[k : k + 1], matrix[k + 1 : k + 2]
        pivot, cross = left[k : k + 1], right[k : k + 1]
        ratio = left[k + 1 : k + 2] / pivot
        new_lower = (lower - ratio * upper) / (right[k + 1 : k + 2] - ratio * cross)
        new_upper = (upper - cross * new_lower) / pivot
        rest = matrix - left * new_upper - right * new_lower
        matrix = jnp.where(row_id == k, new_upper, jnp.where(row_id == k + 1, new_lower, rest))
    return matrix


def local(states, adj_weight, adj_index, partner):
    local_cols, vertices = states.shape
    blocks, _, length, _ = adj_weight.shape
    row_devices, col_devices = lax.axis_size("rows"), lax.axis_size("cols")
    total_cols = local_cols * col_devices
    width = (blocks // 2) * length
    rows = -(-local_cols // 16) * 16
    stages = radices(row_devices)
    field_shape = (2 * blocks, PARTS * rows, length)
    field = pltpu.VMEM(field_shape, jnp.bfloat16)
    full, edge, line = (rows, vertices), (rows, width), (1, vertices)
    slots = (row_devices, rows, length)

    def halves(parity):
        return (
            half(parity, vertices, width, length),
            half(1 - parity, vertices, width, length),
        )

    def edges(index, value, outer, inner):
        at_outer, at_inner = halves(parity_of(index))
        outer[...] = value[:, at_outer]
        inner[...] = value[:, at_inner]

    def first_body(index, weight, outer_states, inner_states, *refs):
        peers, (payload, image, sent, scaled, outer, inner, degree, ones_field) = (
            refs[:col_devices],
            refs[col_devices:],
        )
        parity = parity_of(index)
        at_inner, at_outer = halves(parity)
        fill_extended(
            ones_field,
            parity,
            padded(outer_states[:, at_outer], rows),
            padded(peers[0][...], rows),
            padded(inner_states[:, at_inner], rows),
            length,
        )
        ones_field[:, PARTS * rows :, :] = jnp.ones((2 * blocks, 16, length), jnp.bfloat16)
        payload[...] = jnp.zeros(payload.shape, F32)

        def one(block):
            total = neighbours(index, weight, ones_field, block)
            here = total[PARTS * rows : PARTS * rows + 1]
            value = folded(total, rows)
            at = lanes(block, length)
            degree[:, at] = here
            payload[pl.ds(total_cols + block, 1), :] = here
            image[:, at] = value
            scaled[:, at] = value / here

        each(blocks, one)
        everyone = jnp.concatenate([peer[...] for peer in peers], axis=0)
        other = jnp.concatenate([everyone * degree[...], image[...]], axis=0)
        payload[:total_cols, : total_cols + rows] = lax.dot_general(
            everyone, other, (((1,), (1,)), ((), ())), precision=EXACT, preferred_element_type=F32
        )
        sent[...] = image[:local_cols, :]
        edges(index, scaled, outer, inner)

    def second_body(index, weight, outer, inner, scaled, image, offset, spread):
        fill_extended(spread, parity_of(index), outer[...], scaled[...], inner[...], length)

        def one(block):
            at = lanes(block, length)
            value = folded(neighbours(index, weight, spread, block), rows)
            offset[:, at] = KEEP * image[:, at] + DAMPING * value

        each(blocks, one)

    def ritz_body(index, mates, *refs):
        pieces, refs = refs[: stages[-1]], refs[stages[-1] :]
        peers, refs = refs[:col_devices], refs[col_devices:]
        images, refs = refs[:col_devices], refs[col_devices:]
        own_image, scaled, offset, degree, out, remain, residual, presmooth, pair_degree, table = refs
        group = row_devices // stages[-1] * blocks
        total = pieces[0][:total_cols, :]
        for piece in pieces[1:]:
            total = total + piece[:total_cols, :]
        for place, piece in enumerate(pieces):
            table[place * group : (place + 1) * group, :] = piece[total_cols:, :]
        ritz = jnp.transpose(solved(total, total_cols))[total_cols : total_cols + rows]
        everyone = jnp.concatenate([peer[...] for peer in peers], axis=0)
        spread = jnp.concatenate([image[...] for image in images], axis=0)
        mixed = jnp.dot(ritz, everyone, precision=EXACT, preferred_element_type=F32)
        mixed_image = jnp.dot(ritz, spread, precision=EXACT, preferred_element_type=F32)
        weighted = degree[...] * mixed
        residual[...] = weighted - own_image[...]
        presmooth[...] = DAMPING * (mixed - scaled[...])
        remain[...] = KEEP * weighted + DAMPING * mixed_image - offset[...]
        me = lax.div(index[0, 0], blocks)

        def one(block):
            at = lanes(block, length)
            owner = lax.div(mates[block], blocks)
            row = lax.bitwise_xor(owner, me) * blocks + (mates[block] - owner * blocks)
            out[owner] = remain[:, at]
            pair_degree[:, at] = degree[:, at] + table[pl.ds(row, 1), :]

        each(blocks, one)

    def coarse_body(index, mates, arrived, remain, pair_degree, coarse, fix, outer, inner):
        def one(block):
            at = lanes(block, length)
            value = remain[:, at] + arrived[lax.div(mates[block], blocks)]
            coarse[:, at] = value
            fix[:, at] = DAMPING * value / pair_degree[:, at]

        each(blocks, one)
        edges(index, fix, outer, inner)

    def product_body(index, mates, weight, outer, inner, fix, degree, out, product, spread):
        fill_extended(spread, parity_of(index), outer[...], fix[...], inner[...], length)

        def one(block):
            at = lanes(block, length)
            value = degree[:, at] * fix[:, at] - folded(neighbours(index, weight, spread, block), rows)
            product[:, at] = value
            out[lax.div(mates[block], blocks)] = value

        each(blocks, one)

    def fix_body(
        index, mates, arrived, product, coarse, fix, pair_degree, presmooth, second, outer, inner
    ):
        def one(block):
            at = lanes(block, length)
            image = product[:, at] + arrived[lax.div(mates[block], blocks)]
            step = DAMPING * (coarse[:, at] - image) / pair_degree[:, at]
            second[:, at] = presmooth[:, at] + (fix[:, at] + step)

        each(blocks, one)
        edges(index, second, outer, inner)

    def smooth_body(
        index, weight, outer, inner, second, residual, degree, smooth, squares, spread
    ):
        fill_extended(spread, parity_of(index), outer[...], second[...], inner[...], length)

        def one(block):
            at = lanes(block, length)
            value, here = second[:, at], degree[:, at]
            image = here * value - folded(neighbours(index, weight, spread, block), rows)
            smooth[:, at] = value + DAMPING * (residual[:, at] - image) / here

        each(blocks, one)
        value = smooth[...]
        squares[...] = jnp.broadcast_to(jnp.sum(value * value, axis=1, keepdims=True), squares.shape)

    def scale_body(*refs):
        smooth, correction = refs[-2:]
        total = refs[0][...]
        for piece in refs[1:-2]:
            total = total + piece[...]
        norm = jnp.sqrt(total[:local_cols, :1] / (vertices * row_devices) + EPSILON)
        correction[...] = smooth[:local_cols, :] / norm

    outer, inner = from_pairs(states, states, "rows")
    peers = exchanged(states, "cols", 1, col_devices)
    payload, image, sent, scaled, outer, inner, degree = kernel_call(
        first_body,
        "image",
        [(total_cols + blocks, length), full, (local_cols, vertices), full, edge, edge, line],
        [adj_index],
        [adj_weight, outer, inner, *peers],
        [pltpu.VMEM((2 * blocks, PARTS * rows + 16, length), jnp.bfloat16)],
    )
    stride = 1
    for place, radix in enumerate(stages):
        pieces = exchanged(payload, "rows", stride, radix)
        stride *= radix
        if place + 1 < len(stages):
            summed = pieces[0][:total_cols]
            for piece in pieces[1:]:
                summed = summed + piece[:total_cols]
            payload = jnp.concatenate([summed] + [piece[total_cols:] for piece in pieces], axis=0)
    outer, inner = from_pairs(inner, outer, "rows")
    images = exchanged(sent, "cols", 1, col_devices)
    (offset,) = kernel_call(
        second_body, "offset", [full], [adj_index], [adj_weight, outer, inner, scaled, image], [field]
    )
    out, remain, residual, presmooth, pair_degree = kernel_call(
        ritz_body,
        "ritz",
        [slots, full, full, full, line],
        [adj_index, partner],
        [*pieces, *peers, *images, image, scaled, offset, degree],
        [pltpu.VMEM((row_devices * blocks, length), F32)],
    )
    arrived = lax.all_to_all(out, "rows", split_axis=0, concat_axis=0, tiled=True)
    coarse, fix, outer, inner = kernel_call(
        coarse_body, "coarse", [full, full, edge, edge], [adj_index, partner], [arrived, remain, pair_degree]
    )
    outer, inner = from_pairs(inner, outer, "rows")
    out, product = kernel_call(
        product_body,
        "product",
        [slots, full],
        [adj_index, partner],
        [adj_weight, outer, inner, fix, degree],
        [field],
    )
    arrived = lax.all_to_all(out, "rows", split_axis=0, concat_axis=0, tiled=True)
    second, outer, inner = kernel_call(
        fix_body,
        "fix",
        [full, edge, edge],
        [adj_index, partner],
        [arrived, product, coarse, fix, pair_degree, presmooth],
    )
    outer, inner = from_pairs(inner, outer, "rows")
    smooth, squares = kernel_call(
        smooth_body,
        "smooth",
        [full, (rows, length)],
        [adj_index],
        [adj_weight, outer, inner, second, residual, degree],
        [field],
    )
    stride = 1
    for place, radix in enumerate(stages):
        pieces = exchanged(squares, "rows", stride, radix)
        stride *= radix
        if place + 1 < len(stages):
            squares = pieces[0]
            for piece in pieces[1:]:
                squares = squares + piece
    (correction,) = kernel_call(scale_body, "scale", [states.shape], [], [*pieces, smooth])
    return correction


def solution(mesh):
    return jax.shard_map(
        local,
        mesh=mesh,
        in_specs=(P("cols", "rows"), P("rows", None, None, None), P("rows", None), P("rows")),
        out_specs=P("cols", "rows"),
        check_vma=False,
    )
```

```python
import jax
import jax.numpy as jnp
from jax import lax
from jax.experimental import pallas as pl
from jax.experimental.pallas import tpu as pltpu
from jax.sharding import PartitionSpec as P

DAMPING = 2.0 / 3.0
KEEP = 1.0 - DAMPING
EPSILON = 1e-06
EXACT = lax.Precision.HIGHEST
PARTS = 3
VMEM_GRANT = 16 * 1024 * 1024
F32 = jnp.float32
IN_VMEM = pl.BlockSpec(memory_space=pltpu.VMEM)
IN_SMEM = pl.BlockSpec(memory_space=pltpu.SMEM)


def kernel_call(body, outs, scalars, arrays, scratch=(), cost=2_000_000):
    return pl.pallas_call(
        body,
        out_shape=[
            out if isinstance(out, jax.ShapeDtypeStruct) else jax.ShapeDtypeStruct(out, F32)
            for out in outs
        ],
        in_specs=[IN_SMEM] * len(scalars) + [IN_VMEM] * len(arrays),
        out_specs=[IN_VMEM] * len(outs),
        scratch_shapes=list(scratch),
        compiler_params=pltpu.CompilerParams(vmem_limit_bytes=VMEM_GRANT),
        cost_estimate=pl.CostEstimate(flops=cost, bytes_accessed=cost, transcendentals=0),
    )(*scalars, *arrays)


def exchanged(value, axis):
    peers = lax.axis_size(axis)
    return [value] + [
        lax.ppermute(value, axis, [(i, i ^ mask) for i in range(peers)]) for mask in range(1, peers)
    ]


def swapped(value, axis):
    return lax.all_to_all(value, axis, split_axis=0, concat_axis=0, tiled=True)


def across_outer(value, axis):
    peers = lax.axis_size(axis)
    up = [(i, i + 1) for i in range(1, peers - 1, 2)]
    return lax.ppermute(value, axis, up + [(j, i) for i, j in up])


def across_inner(value, axis):
    return lax.ppermute(value, axis, [(i, i ^ 1) for i in range(lax.axis_size(axis))])


def each(count, body):
    if count <= 16:
        for step in range(count):
            body(step)
    else:
        lax.fori_loop(0, count, lambda step, carry: (body(step), carry)[1], 0)


def lanes(block, length):
    start = block * length
    return pl.ds(start if isinstance(block, int) else pl.multiple_of(start, length), length)


def padded(value, rows):
    if value.shape[0] == rows:
        return value
    return jnp.concatenate([value, jnp.zeros((rows - value.shape[0], value.shape[1]), F32)], axis=0)


def in_parts(value):
    pieces = []
    for _ in range(PARTS):
        piece = value.astype(jnp.bfloat16)
        pieces.append(piece)
        value = value - piece.astype(F32)
    return jnp.concatenate(pieces, axis=0)


def fill(field, base, value, length):
    split = in_parts(value)
    for block in range(value.shape[1] // length):
        field[base + block, : split.shape[0], :] = split[:, block * length : (block + 1) * length]


def split(block, blocks):
    if blocks & (blocks - 1):
        return lax.div(block, blocks), lax.rem(block, blocks)
    bits = blocks.bit_length() - 1
    return lax.shift_right_logical(block, bits), lax.bitwise_and(block, blocks - 1)


def parity_of(index):
    return lax.bitwise_and(split(index[0, 0], index.shape[1])[0], 1)


def half(parity, vertices, width, length):
    return pl.ds(pl.multiple_of(parity * (vertices - width), length), width)


def fill_extended(field, parity, outer, own, inner, length):
    margin, blocks = outer.shape[1] // length, own.shape[1] // length
    fill(field, parity * (margin + blocks), outer, length)
    fill(field, margin, own, length)
    fill(field, (1 - parity) * (margin + blocks), inner, length)


def neighbours(index, weight, field, block):
    shift = index.shape[1] // 2 - index[0, 0]
    total = None
    for k in range(index.shape[0]):
        term = lax.dot_general(
            field[index[k, block] + shift],
            weight[block, k],
            (((1,), (1,)), ((), ())),
            preferred_element_type=F32,
        )
        total = term if total is None else total + term
    return total


def folded(total, rows):
    return total[:rows] + total[rows : 2 * rows] + total[2 * rows : PARTS * rows]


def solved(matrix, size):
    row_id = lax.broadcasted_iota(jnp.int32, matrix.shape, 0)
    for k in range(0, size, 2):
        left = jnp.broadcast_to(matrix[:, k : k + 1], matrix.shape)
        right = jnp.broadcast_to(matrix[:, k + 1 : k + 2], matrix.shape)
        upper, lower = matrix[k : k + 1], matrix[k + 1 : k + 2]
        pivot, cross = left[k : k + 1], right[k : k + 1]
        ratio = left[k + 1 : k + 2] / pivot
        new_lower = (lower - ratio * upper) / (right[k + 1 : k + 2] - ratio * cross)
        new_upper = (upper - cross * new_lower) / pivot
        rest = matrix - left * new_upper - right * new_lower
        matrix = jnp.where(row_id == k, new_upper, jnp.where(row_id == k + 1, new_lower, rest))
    return matrix


def local(states, adj_weight, adj_index, partner):
    local_cols, vertices = states.shape
    blocks, _, length, _ = adj_weight.shape
    row_devices, col_devices = lax.axis_size("rows"), lax.axis_size("cols")
    total_cols = local_cols * col_devices
    margin = blocks // 2
    width = margin * length
    rows = -(-local_cols // 16) * 16
    packed_rows = total_cols // 2
    field_shape = (2 * blocks, PARTS * rows, length)
    field = pltpu.VMEM(field_shape, jnp.bfloat16)
    full, edge, line = (rows, vertices), (rows, width), (1, vertices)
    slots = (row_devices, 2 * rows, length)

    def halves(parity):
        return (
            half(parity, vertices, width, length),
            half(1 - parity, vertices, width, length),
        )

    def place(out, mate, value):
        owner, position = split(mate, blocks)
        side = lax.bitwise_and(owner, 1)
        beside = owner + 2 * side - 1
        high = lax.select(position >= margin, 1, 0)
        wanted = (high == side) & (beside >= 0) & (beside < row_devices)
        out[owner, :rows, :] = value
        start = lax.select(wanted, rows, 0)
        target = lax.select(wanted, beside, owner)
        out[target, pl.ds(pl.multiple_of(start, rows), rows), :] = value

    def degree_body(weight, degree):
        ones = jnp.ones((16, length), jnp.bfloat16)

        def one(block):
            total = None
            for k in range(weight.shape[1]):
                term = lax.dot_general(
                    ones,
                    weight[block, k],
                    (((1,), (1,)), ((), ())),
                    preferred_element_type=F32,
                )
                total = term if total is None else total + term
            degree[:, lanes(block, length)] = total[:1]

        each(blocks, one)

    def image_body(index, mates, weight, degree, outer_states, inner_states, states, *refs):
        image, sent, scaled, outer, inner, spread = refs
        parity = parity_of(index)
        at_own_outer, at_own_inner = halves(parity)
        fill_extended(
            spread,
            parity,
            padded(outer_states[:, at_own_inner], rows),
            padded(states[...], rows),
            padded(inner_states[:, at_own_outer], rows),
            length,
        )

        def one(block):
            value = folded(neighbours(index, weight, spread, block), rows)
            at = lanes(block, length)
            image[:, at] = value
            scaled[:, at] = value / degree[:, at]

        each(blocks, one)
        sent[...] = image[:local_cols, :]
        inner[...] = scaled[:, at_own_inner]
        outer[:, :width] = scaled[:, at_own_outer]
        lane = lax.broadcasted_iota(jnp.int32, (rows, length), 1)
        listed = jnp.zeros((rows, length), jnp.int32)
        for block in range(blocks):
            listed = jnp.where(lane == block, mates[block], listed)
        outer[:, width:] = listed.astype(F32)

    def products_body(mates, *refs):
        peers, (image, degree, shared) = refs[:col_devices], refs[col_devices:]
        everyone = jnp.concatenate([peer[...] for peer in peers], axis=0)
        other = jnp.concatenate([everyone * degree[...], image[...]], axis=0)
        products = lax.dot_general(
            everyone,
            padded(other, length),
            (((1,), (1,)), ((), ())),
            precision=EXACT,
            preferred_element_type=F32,
        )
        packed = products[:packed_rows] + pltpu.roll(products[packed_rows:], length // 2, 1)
        for device in range(row_devices):
            shared[device, :packed_rows, :] = packed

        def send_degree(block):
            owner = split(mates[block], blocks)[0]
            shared[owner, packed_rows : packed_rows + 1, :] = degree[:, lanes(block, length)]

        each(blocks, send_degree)

    def ritz_body(index, mates, weight, outer, inner, shared, *refs):
        peers, refs = refs[:col_devices], refs[col_devices:]
        images, refs = refs[:col_devices], refs[col_devices:]
        own_image, scaled, degree, *refs = refs
        out, remain, residual, presmooth, pair_degree, beside, spread_field = refs
        parity = parity_of(index)
        fill_extended(spread_field, parity, outer[:, :width], scaled[...], inner[...], length)

        def offset(block):
            at = lanes(block, length)
            value = folded(neighbours(index, weight, spread_field, block), rows)
            remain[:, at] = KEEP * own_image[:, at] + DAMPING * value

        each(blocks, offset)
        total = shared[0, :packed_rows, :]
        for device in range(1, row_devices):
            total = total + shared[device, :packed_rows, :]
        total = jnp.concatenate([total, pltpu.roll(total, length // 2, 1)], axis=0)
        ritz = jnp.transpose(solved(total, total_cols))[total_cols : total_cols + rows]
        everyone = jnp.concatenate([peer[...] for peer in peers], axis=0)
        spread = jnp.concatenate([image[...] for image in images], axis=0)
        mixed = jnp.dot(ritz, everyone, precision=EXACT, preferred_element_type=F32)
        mixed_image = jnp.dot(ritz, spread, precision=EXACT, preferred_element_type=F32)
        weighted = degree[...] * mixed
        residual[...] = weighted - own_image[...]
        presmooth[...] = DAMPING * (mixed - scaled[...])
        remain[...] = KEEP * weighted + DAMPING * mixed_image - remain[...]

        def one(block):
            at = lanes(block, length)
            place(out, mates[block], remain[:, at])
            other = shared[split(mates[block], blocks)[0], packed_rows : packed_rows + 1, :]
            pair_degree[:, at] = degree[:, at] + other

        each(blocks, one)
        at_outer, _ = halves(parity)
        beside[:, :width] = remain[:, at_outer]
        beside[:, width:] = jnp.zeros((rows, length), F32)
        shared_degree = pair_degree[:, at_outer]
        for block in range(margin):
            beside[block : block + 1, width:] = shared_degree[:, block * length : (block + 1) * length]

    def beside_slot(index, outer_mates, block):
        return split(outer_mates[(1 - parity_of(index)) * margin + block], blocks)[0]

    def coarse_body(
        index, mates, outer_mates, arrived, beside, remain, pair_degree, coarse, fix, further, inner
    ):
        def one(block):
            at = lanes(block, length)
            value = remain[:, at] + arrived[split(mates[block], blocks)[0], :rows, :]
            coarse[:, at] = value
            fix[:, at] = DAMPING * value / pair_degree[:, at]

        def other(block):
            at = lanes(block, length)
            source = beside_slot(index, outer_mates, block)
            value = beside[:, at] + arrived[source, rows:, :]
            further[:rows, at] = DAMPING * value / beside[pl.ds(block, 1), width:]
            further[rows:, at] = value

        each(blocks, one)
        each(margin, other)
        inner[...] = fix[:, halves(parity_of(index))[1]]

    def product_body(
        index, mates, weight, further, inner, fix, degree, presmooth, pair_degree, *refs
    ):
        out, product, outer, spread = refs
        fill_extended(spread, parity_of(index), further[:rows, :], fix[...], inner[...], length)

        def one(block):
            at = lanes(block, length)
            value = degree[:, at] * fix[:, at] - folded(neighbours(index, weight, spread, block), rows)
            product[:, at] = value

        each(blocks, one)
        each(blocks, lambda block: place(out, mates[block], product[:, lanes(block, length)]))
        at_outer, _ = halves(parity_of(index))
        step = DAMPING * product[:, at_outer] / pair_degree[:, at_outer]
        outer[...] = presmooth[:, at_outer] - step

    def fix_body(index, mates, outer_mates, arrived, partial, beside, further, *refs):
        product, coarse, fix, pair_degree, presmooth, second, outer, inner = refs

        def one(block):
            at = lanes(block, length)
            image = product[:, at] + arrived[split(mates[block], blocks)[0], :rows, :]
            step = DAMPING * (coarse[:, at] - image) / pair_degree[:, at]
            second[:, at] = presmooth[:, at] + (fix[:, at] + step)

        def other(block):
            at = lanes(block, length)
            source = beside_slot(index, outer_mates, block)
            image = further[rows:, at] - arrived[source, rows:, :]
            step = DAMPING * image / beside[pl.ds(block, 1), width:]
            outer[:, at] = partial[:, at] + (further[:rows, at] + step)

        each(blocks, one)
        each(margin, other)
        inner[...] = second[:, halves(parity_of(index))[1]]

    def smooth_body(
        index, weight, outer, inner, second, residual, degree, smooth, squares, spread
    ):
        fill_extended(spread, parity_of(index), outer[...], second[...], inner[...], length)

        def one(block):
            at = lanes(block, length)
            value, here = second[:, at], degree[:, at]
            image = here * value - folded(neighbours(index, weight, spread, block), rows)
            smooth[:, at] = value + DAMPING * (residual[:, at] - image) / here

        each(blocks, one)
        value = smooth[...]
        total = jnp.broadcast_to(jnp.sum(value * value, axis=1, keepdims=True), (rows, length))
        lane = lax.broadcasted_iota(jnp.int32, (rows // 2, length), 1)
        packed = jnp.where(lane < length // 2, total[: rows // 2], total[rows // 2 :])
        for device in range(row_devices):
            squares[device] = packed

    def scale_body(squares, smooth, correction):
        total = squares[0]
        for device in range(1, row_devices):
            total = total + squares[device]
        total = jnp.concatenate([total, pltpu.roll(total, length // 2, 1)], axis=0)
        norm = jnp.sqrt(total[:local_cols, :1] / (vertices * row_devices) + EPSILON)
        correction[...] = smooth[:local_cols, :] / norm

    adj_index = adj_index.T
    outer = across_outer(states, "rows")
    inner = across_inner(states, "rows")
    peers = exchanged(states, "cols")
    (degree,) = kernel_call(degree_body, [line], [], [adj_weight])
    image, sent, scaled, outer, inner = kernel_call(
        image_body,
        [full, (local_cols, vertices), full, (rows, width + length), edge],
        [adj_index, partner],
        [adj_weight, degree, outer, inner, states],
        [field],
    )
    (shared,) = kernel_call(
        products_body, [(row_devices, packed_rows + 8, length)], [partner], [*peers, image, degree]
    )
    shared = swapped(shared, "rows")
    outer = across_outer(outer, "rows")
    inner = across_inner(inner, "rows")
    images = exchanged(sent, "cols")
    outer_mates = outer[0, width : width + blocks].astype(jnp.int32)
    out, remain, residual, presmooth, pair_degree, beside = kernel_call(
        ritz_body,
        [slots, full, full, full, line, (rows, width + length)],
        [adj_index, partner],
        [adj_weight, outer, inner, shared, *peers, *images, image, scaled, degree],
        [field],
    )
    arrived = swapped(out, "rows")
    beside = across_outer(beside, "rows")
    coarse, fix, further, inner = kernel_call(
        coarse_body,
        [full, full, (2 * rows, width), edge],
        [adj_index, partner, outer_mates],
        [arrived, beside, remain, pair_degree],
    )
    inner = across_inner(inner, "rows")
    out, product, outer = kernel_call(
        product_body,
        [slots, full, edge],
        [adj_index, partner],
        [adj_weight, further, inner, fix, degree, presmooth, pair_degree],
        [field],
    )
    arrived = swapped(out, "rows")
    outer = across_outer(outer, "rows")
    second, outer, inner = kernel_call(
        fix_body,
        [full, edge, edge],
        [adj_index, partner, outer_mates],
        [arrived, outer, beside, further, product, coarse, fix, pair_degree, presmooth],
    )
    inner = across_inner(inner, "rows")
    smooth, squares = kernel_call(
        smooth_body,
        [full, (row_devices, rows // 2, length)],
        [adj_index],
        [adj_weight, outer, inner, second, residual, degree],
        [field],
    )
    squares = swapped(squares, "rows")
    (correction,) = kernel_call(scale_body, [states.shape], [], [squares, smooth])
    return correction


def solution(mesh):
    return jax.shard_map(
        local,
        mesh=mesh,
        in_specs=(P("cols", "rows"), P("rows", None, None, None), P("rows", None), P("rows")),
        out_specs=P("cols", "rows"),
        check_vma=False,
    )
```

```python
import jax
import jax.numpy as jnp
from jax import lax
from jax.experimental import pallas as pl
from jax.experimental.pallas import tpu as pltpu
from jax.sharding import PartitionSpec as P

DAMPING = 2.0 / 3.0
KEEP = 1.0 - DAMPING
EPSILON = 1e-06
EXACT = lax.Precision.HIGHEST
PARTS = 3
VMEM_GRANT = 16 * 1024 * 1024
F32 = jnp.float32
IN_VMEM = pl.BlockSpec(memory_space=pltpu.VMEM)
IN_SMEM = pl.BlockSpec(memory_space=pltpu.SMEM)


def kernel_call(body, outs, scalars, arrays, scratch=(), cost=2_000_000):
    return pl.pallas_call(
        body,
        out_shape=[
            out if isinstance(out, jax.ShapeDtypeStruct) else jax.ShapeDtypeStruct(out, F32)
            for out in outs
        ],
        in_specs=[IN_SMEM] * len(scalars) + [IN_VMEM] * len(arrays),
        out_specs=[IN_VMEM] * len(outs),
        scratch_shapes=list(scratch),
        compiler_params=pltpu.CompilerParams(vmem_limit_bytes=VMEM_GRANT),
        cost_estimate=pl.CostEstimate(flops=cost, bytes_accessed=cost, transcendentals=0),
    )(*scalars, *arrays)


def exchanged(value, axis):
    peers = lax.axis_size(axis)
    return [value] + [
        lax.ppermute(value, axis, [(i, i ^ mask) for i in range(peers)]) for mask in range(1, peers)
    ]


def swapped(value, axis):
    return lax.all_to_all(value, axis, split_axis=0, concat_axis=0, tiled=True)


def across_outer(value, axis):
    peers = lax.axis_size(axis)
    up = [(i, i + 1) for i in range(1, peers - 1, 2)]
    return lax.ppermute(value, axis, up + [(j, i) for i, j in up])


def across_inner(value, axis):
    return lax.ppermute(value, axis, [(i, i ^ 1) for i in range(lax.axis_size(axis))])


def each(count, body):
    if count <= 16:
        for step in range(count):
            body(step)
    else:
        lax.fori_loop(0, count, lambda step, carry: (body(step), carry)[1], 0)


def lanes(block, length):
    start = block * length
    return pl.ds(start if isinstance(block, int) else pl.multiple_of(start, length), length)


def padded(value, rows):
    if value.shape[0] == rows:
        return value
    return jnp.concatenate([value, jnp.zeros((rows - value.shape[0], value.shape[1]), F32)], axis=0)


def in_parts(value):
    pieces = []
    for _ in range(PARTS):
        piece = value.astype(jnp.bfloat16)
        pieces.append(piece)
        value = value - piece.astype(F32)
    return jnp.concatenate(pieces, axis=0)


def fill(field, base, value, length):
    split = in_parts(value)
    for block in range(value.shape[1] // length):
        field[base + block, : split.shape[0], :] = split[:, block * length : (block + 1) * length]


def split(block, blocks):
    if blocks & (blocks - 1):
        return lax.div(block, blocks), lax.rem(block, blocks)
    bits = blocks.bit_length() - 1
    return lax.shift_right_logical(block, bits), lax.bitwise_and(block, blocks - 1)


def parity_of(index):
    return lax.bitwise_and(split(index[0, 0], index.shape[1])[0], 1)


def half(parity, vertices, width, length):
    return pl.ds(pl.multiple_of(parity * (vertices - width), length), width)


def fill_extended(field, parity, outer, own, inner, length):
    margin, blocks = outer.shape[1] // length, own.shape[1] // length
    fill(field, parity * (margin + blocks), outer, length)
    fill(field, margin, own, length)
    fill(field, (1 - parity) * (margin + blocks), inner, length)


def neighbours(index, weight, field, block):
    shift = index.shape[1] // 2 - index[0, 0]
    total = None
    for k in range(index.shape[0]):
        term = lax.dot_general(
            field[index[k, block] + shift],
            weight[block, k],
            (((1,), (1,)), ((), ())),
            preferred_element_type=F32,
        )
        total = term if total is None else total + term
    return total


def folded(total, rows):
    return total[:rows] + total[rows : 2 * rows] + total[2 * rows : PARTS * rows]


def solved(matrix, size):
    row_id = lax.broadcasted_iota(jnp.int32, matrix.shape, 0)
    step = 8 if size % 8 == 0 else 1
    for base in range(0, size, step):
        ids = range(step)
        columns = [
            jnp.broadcast_to(matrix[:, base + j : base + j + 1], matrix.shape) for j in ids
        ]
        block = [[columns[j][base + i : base + i + 1] for j in ids] for i in ids]
        lines = [matrix[base + i : base + i + 1] for i in ids]
        for i in ids:
            scale = 1.0 / block[i][i]
            lines[i] = lines[i] * scale
            for j in range(i + 1, step):
                block[i][j] = block[i][j] * scale
            for other in ids:
                if other == i:
                    continue
                factor = block[other][i]
                lines[other] = lines[other] - factor * lines[i]
                for j in range(i + 1, step):
                    block[other][j] = block[other][j] - factor * block[i][j]
        for j in ids:
            matrix = matrix - columns[j] * lines[j]
        for j in ids:
            matrix = jnp.where(row_id == base + j, lines[j], matrix)
    return matrix


def local(states, adj_weight, adj_index, partner):
    local_cols, vertices = states.shape
    blocks, _, length, _ = adj_weight.shape
    row_devices, col_devices = lax.axis_size("rows"), lax.axis_size("cols")
    total_cols = local_cols * col_devices
    margin = blocks // 2
    width = margin * length
    rows = -(-local_cols // 16) * 16
    packed_rows = total_cols // 2
    field_shape = (2 * blocks, PARTS * rows, length)
    field = pltpu.VMEM(field_shape, jnp.bfloat16)
    full, edge, line = (rows, vertices), (rows, width), (1, vertices)
    slots = (2 * row_devices, rows, length)

    def halves(parity):
        return (
            half(parity, vertices, width, length),
            half(1 - parity, vertices, width, length),
        )

    def place(out, mate, value):
        owner, position = split(mate, blocks)
        side = lax.bitwise_and(owner, 1)
        beside = owner + 2 * side - 1
        high = lax.select(position >= margin, 1, 0)
        wanted = (high == side) & (beside >= 0) & (beside < row_devices)
        out[2 * owner] = value
        out[lax.select(wanted, 2 * beside + 1, 2 * owner)] = value

    def ones_body(ones):
        ones[...] = jnp.ones(ones.shape, ones.dtype)

    def degree_body(ones, weight, degree, degrees):
        def one(block):
            total = None
            for k in range(weight.shape[1]):
                term = lax.dot_general(
                    ones[...],
                    weight[block, k],
                    (((1,), (1,)), ((), ())),
                    preferred_element_type=F32,
                )
                total = term if total is None else total + term
            degree[:, lanes(block, length)] = total[:1]
            degrees[pl.ds(block, 1), :] = total[:1]

        each(blocks, one)

    def image_body(index, mates, weight, degree, outer_states, inner_states, states, *refs):
        image, sent, scaled, outer, inner, spread = refs
        parity = parity_of(index)
        at_own_outer, at_own_inner = halves(parity)
        fill_extended(
            spread,
            parity,
            padded(outer_states[:, at_own_inner], rows),
            padded(states[...], rows),
            padded(inner_states[:, at_own_outer], rows),
            length,
        )

        def one(block):
            value = folded(neighbours(index, weight, spread, block), rows)
            at = lanes(block, length)
            image[:, at] = value
            scaled[:, at] = value / degree[:, at]

        each(blocks, one)
        sent[...] = image[:local_cols, :]
        inner[...] = scaled[:, at_own_inner]
        outer[:, :width] = scaled[:, at_own_outer]
        lane = lax.broadcasted_iota(jnp.int32, (rows, length), 1)
        listed = jnp.zeros((rows, length), jnp.int32)
        for block in range(blocks):
            listed = jnp.where(lane == block, mates[block], listed)
        outer[:, width:] = listed.astype(F32)

    def products_body(*refs):
        peers, (image, degree, degrees, shared, wide) = refs[:col_devices], refs[col_devices:]
        everyone = jnp.concatenate([peer[...] for peer in peers], axis=0)
        other = jnp.concatenate([everyone * degree[...], image[...]], axis=0)
        wide[...] = jnp.zeros(wide.shape, F32)
        wide[:, : total_cols + rows] = lax.dot_general(
            everyone,
            other,
            (((1,), (1,)), ((), ())),
            precision=EXACT,
            preferred_element_type=F32,
        )
        packed = wide[:packed_rows, :] + pltpu.roll(wide[packed_rows:, :], length // 2, 1)
        for device in range(row_devices):
            shared[device, :packed_rows, :] = packed
            shared[device, packed_rows:, :] = degrees[...]

    def ritz_body(index, mates, weight, outer, inner, shared, *refs):
        peers, refs = refs[:col_devices], refs[col_devices:]
        images, refs = refs[:col_devices], refs[col_devices:]
        own_image, scaled, degree, *refs = refs
        out, remain, residual, presmooth, pair_degree, beside, spread_field = refs
        parity = parity_of(index)
        fill_extended(spread_field, parity, outer[:, :width], scaled[...], inner[...], length)

        def offset(block):
            at = lanes(block, length)
            value = folded(neighbours(index, weight, spread_field, block), rows)
            remain[:, at] = KEEP * own_image[:, at] + DAMPING * value

        each(blocks, offset)
        total = shared[0, :packed_rows, :]
        for device in range(1, row_devices):
            total = total + shared[device, :packed_rows, :]
        total = jnp.concatenate([total, pltpu.roll(total, length // 2, 1)], axis=0)
        ritz = jnp.transpose(solved(total, total_cols))[total_cols : total_cols + rows]
        everyone = jnp.concatenate([peer[...] for peer in peers], axis=0)
        spread = jnp.concatenate([image[...] for image in images], axis=0)
        mixed = jnp.dot(ritz, everyone, precision=EXACT, preferred_element_type=F32)
        mixed_image = jnp.dot(ritz, spread, precision=EXACT, preferred_element_type=F32)
        weighted = degree[...] * mixed
        residual[...] = weighted - own_image[...]
        presmooth[...] = DAMPING * (mixed - scaled[...])
        remain[...] = KEEP * weighted + DAMPING * mixed_image - remain[...]

        def one(block):
            at = lanes(block, length)
            place(out, mates[block], remain[:, at])
            owner, position = split(mates[block], blocks)
            pair_degree[:, at] = degree[:, at] + shared[owner, pl.ds(packed_rows + position, 1), :]

        each(blocks, one)
        at_outer, _ = halves(parity)
        beside[:, :width] = remain[:, at_outer]
        beside[:, width:] = jnp.zeros((rows, length), F32)
        shared_degree = pair_degree[:, at_outer]
        for block in range(margin):
            beside[block : block + 1, width:] = shared_degree[:, block * length : (block + 1) * length]

    def beside_slot(index, outer_mates, block):
        return split(outer_mates[(1 - parity_of(index)) * margin + block], blocks)[0]

    def coarse_body(
        index, mates, outer_mates, arrived, beside, remain, pair_degree, coarse, fix, further, inner
    ):
        def one(block):
            at = lanes(block, length)
            value = remain[:, at] + arrived[2 * split(mates[block], blocks)[0]]
            coarse[:, at] = value
            fix[:, at] = DAMPING * value / pair_degree[:, at]

        def other(block):
            at = lanes(block, length)
            source = beside_slot(index, outer_mates, block)
            value = beside[:, at] + arrived[2 * source + 1]
            further[:rows, at] = DAMPING * value / beside[pl.ds(block, 1), width:]
            further[rows:, at] = value

        each(blocks, one)
        each(margin, other)
        inner[...] = fix[:, halves(parity_of(index))[1]]

    def product_body(
        index, mates, weight, further, inner, fix, degree, presmooth, pair_degree, *refs
    ):
        out, product, outer, spread = refs
        fill_extended(spread, parity_of(index), further[:rows, :], fix[...], inner[...], length)

        def one(block):
            at = lanes(block, length)
            value = degree[:, at] * fix[:, at] - folded(neighbours(index, weight, spread, block), rows)
            product[:, at] = value

        each(blocks, one)
        each(blocks, lambda block: place(out, mates[block], product[:, lanes(block, length)]))
        at_outer, _ = halves(parity_of(index))
        step = DAMPING * product[:, at_outer] / pair_degree[:, at_outer]
        outer[...] = presmooth[:, at_outer] - step

    def fix_body(index, mates, outer_mates, arrived, partial, beside, further, *refs):
        product, coarse, fix, pair_degree, presmooth, second, outer, inner = refs

        def one(block):
            at = lanes(block, length)
            image = product[:, at] + arrived[2 * split(mates[block], blocks)[0]]
            step = DAMPING * (coarse[:, at] - image) / pair_degree[:, at]
            second[:, at] = presmooth[:, at] + (fix[:, at] + step)

        def other(block):
            at = lanes(block, length)
            source = beside_slot(index, outer_mates, block)
            image = further[rows:, at] - arrived[2 * source + 1]
            step = DAMPING * image / beside[pl.ds(block, 1), width:]
            outer[:, at] = partial[:, at] + (further[:rows, at] + step)

        each(blocks, one)
        each(margin, other)
        inner[...] = second[:, halves(parity_of(index))[1]]

    def smooth_body(
        index, weight, outer, inner, second, residual, degree, smooth, squares, spread
    ):
        fill_extended(spread, parity_of(index), outer[...], second[...], inner[...], length)

        def one(block):
            at = lanes(block, length)
            value, here = second[:, at], degree[:, at]
            image = here * value - folded(neighbours(index, weight, spread, block), rows)
            smooth[:, at] = value + DAMPING * (residual[:, at] - image) / here

        each(blocks, one)
        value = smooth[...]
        total = jnp.broadcast_to(jnp.sum(value * value, axis=1, keepdims=True), (rows, length))
        lane = lax.broadcasted_iota(jnp.int32, (rows // 2, length), 1)
        packed = jnp.where(lane < length // 2, total[: rows // 2], total[rows // 2 :])
        for device in range(row_devices):
            squares[device] = packed

    def scale_body(squares, smooth, correction):
        total = squares[0]
        for device in range(1, row_devices):
            total = total + squares[device]
        total = jnp.concatenate([total, pltpu.roll(total, length // 2, 1)], axis=0)
        norm = jnp.sqrt(total[:local_cols, :1] / (vertices * row_devices) + EPSILON)
        correction[...] = smooth[:local_cols, :] / norm

    adj_index = adj_index.T
    outer = across_outer(states, "rows")
    inner = across_inner(states, "rows")
    peers = exchanged(states, "cols")
    ones_shape = jax.ShapeDtypeStruct((16, length), jnp.bfloat16)
    (ones,) = kernel_call(ones_body, [ones_shape], [], [], cost=20_000_000_000)
    degree, degrees = kernel_call(degree_body, [line, (blocks, length)], [], [ones, adj_weight])
    image, sent, scaled, outer, inner = kernel_call(
        image_body,
        [full, (local_cols, vertices), full, (rows, width + length), edge],
        [adj_index, partner],
        [adj_weight, degree, outer, inner, states],
        [field],
    )
    (shared,) = kernel_call(
        products_body,
        [(row_devices, packed_rows + blocks, length)],
        [],
        [*peers, image, degree, degrees],
        [pltpu.VMEM((total_cols, length), F32)],
    )
    shared = swapped(shared, "rows")
    outer = across_outer(outer, "rows")
    inner = across_inner(inner, "rows")
    images = exchanged(sent, "cols")
    outer_mates = outer[0, width : width + blocks].astype(jnp.int32)
    out, remain, residual, presmooth, pair_degree, beside = kernel_call(
        ritz_body,
        [slots, full, full, full, line, (rows, width + length)],
        [adj_index, partner],
        [adj_weight, outer, inner, shared, *peers, *images, image, scaled, degree],
        [field],
    )
    arrived = swapped(out, "rows")
    beside = across_outer(beside, "rows")
    coarse, fix, further, inner = kernel_call(
        coarse_body,
        [full, full, (2 * rows, width), edge],
        [adj_index, partner, outer_mates],
        [arrived, beside, remain, pair_degree],
    )
    inner = across_inner(inner, "rows")
    out, product, outer = kernel_call(
        product_body,
        [slots, full, edge],
        [adj_index, partner],
        [adj_weight, further, inner, fix, degree, presmooth, pair_degree],
        [field],
    )
    arrived = swapped(out, "rows")
    outer = across_outer(outer, "rows")
    second, outer, inner = kernel_call(
        fix_body,
        [full, edge, edge],
        [adj_index, partner, outer_mates],
        [arrived, outer, beside, further, product, coarse, fix, pair_degree, presmooth],
    )
    inner = across_inner(inner, "rows")
    smooth, squares = kernel_call(
        smooth_body,
        [full, (row_devices, rows // 2, length)],
        [adj_index],
        [adj_weight, outer, inner, second, residual, degree],
        [field],
    )
    squares = swapped(squares, "rows")
    (correction,) = kernel_call(scale_body, [states.shape], [], [squares, smooth])
    return correction


def solution(mesh):
    return jax.shard_map(
        local,
        mesh=mesh,
        in_specs=(P("cols", "rows"), P("rows", None, None, None), P("rows", None), P("rows")),
        out_specs=P("cols", "rows"),
        check_vma=False,
    )
```

```python
import jax
import jax.numpy as jnp
from jax import lax
from jax.experimental import pallas as pl
from jax.experimental.pallas import tpu as pltpu
from jax.sharding import PartitionSpec as P

DAMPING = 2.0 / 3.0
KEEP = 1.0 - DAMPING
EPSILON = 1e-06
EXACT = lax.Precision.HIGHEST
PARTS = 3
VMEM_GRANT = 16 * 1024 * 1024
F32 = jnp.float32
IN_VMEM = pl.BlockSpec(memory_space=pltpu.VMEM)
IN_SMEM = pl.BlockSpec(memory_space=pltpu.SMEM)


def kernel_call(body, outs, scalars, arrays, scratch=(), cost=2_000_000):
    return pl.pallas_call(
        body,
        out_shape=[
            out if isinstance(out, jax.ShapeDtypeStruct) else jax.ShapeDtypeStruct(out, F32)
            for out in outs
        ],
        in_specs=[IN_SMEM] * len(scalars) + [IN_VMEM] * len(arrays),
        out_specs=[IN_VMEM] * len(outs),
        scratch_shapes=list(scratch),
        compiler_params=pltpu.CompilerParams(vmem_limit_bytes=VMEM_GRANT),
        cost_estimate=pl.CostEstimate(flops=cost, bytes_accessed=cost, transcendentals=0),
    )(*scalars, *arrays)


def exchanged(value, axis):
    peers = lax.axis_size(axis)
    return [value] + [
        lax.ppermute(value, axis, [(i, i ^ mask) for i in range(peers)]) for mask in range(1, peers)
    ]


def swapped(value, axis):
    return lax.all_to_all(value, axis, split_axis=0, concat_axis=0, tiled=True)


def across_outer(value, axis):
    peers = lax.axis_size(axis)
    up = [(i, i + 1) for i in range(1, peers - 1, 2)]
    return lax.ppermute(value, axis, up + [(j, i) for i, j in up])


def across_inner(value, axis):
    return lax.ppermute(value, axis, [(i, i ^ 1) for i in range(lax.axis_size(axis))])


def each(count, body):
    if count <= 16:
        for step in range(count):
            body(step)
    else:
        lax.fori_loop(0, count, lambda step, carry: (body(step), carry)[1], 0)


def lanes(block, length):
    start = block * length
    return pl.ds(start if isinstance(block, int) else pl.multiple_of(start, length), length)


def padded(value, rows):
    if value.shape[0] == rows:
        return value
    return jnp.concatenate([value, jnp.zeros((rows - value.shape[0], value.shape[1]), F32)], axis=0)


def in_parts(value):
    pieces = []
    for _ in range(PARTS):
        piece = value.astype(jnp.bfloat16)
        pieces.append(piece)
        value = value - piece.astype(F32)
    return jnp.concatenate(pieces, axis=0)


def fill(field, base, value, length):
    split = in_parts(value)
    for block in range(value.shape[1] // length):
        field[base + block, : split.shape[0], :] = split[:, block * length : (block + 1) * length]


def split(block, blocks):
    if blocks & (blocks - 1):
        return lax.div(block, blocks), lax.rem(block, blocks)
    bits = blocks.bit_length() - 1
    return lax.shift_right_logical(block, bits), lax.bitwise_and(block, blocks - 1)


def parity_of(index):
    return lax.bitwise_and(split(index[0, 0], index.shape[1])[0], 1)


def half(parity, vertices, width, length):
    return pl.ds(pl.multiple_of(parity * (vertices - width), length), width)


def fill_extended(field, parity, outer, own, inner, length):
    margin, blocks = outer.shape[1] // length, own.shape[1] // length
    fill(field, parity * (margin + blocks), outer, length)
    fill(field, margin, own, length)
    fill(field, (1 - parity) * (margin + blocks), inner, length)


def neighbours(index, weight, field, block):
    shift = index.shape[1] // 2 - index[0, 0]
    total = None
    for k in range(index.shape[0]):
        term = lax.dot_general(
            field[index[k, block] + shift],
            weight[block, k],
            (((1,), (1,)), ((), ())),
            preferred_element_type=F32,
        )
        total = term if total is None else total + term
    return total


def folded(total, rows):
    return total[:rows] + total[rows : 2 * rows] + total[2 * rows : PARTS * rows]


def solved(matrix, size):
    row_id = lax.broadcasted_iota(jnp.int32, matrix.shape, 0)
    step = 8 if size % 8 == 0 else 1
    for base in range(0, size, step):
        ids = range(step)
        columns = [
            jnp.broadcast_to(matrix[:, base + j : base + j + 1], matrix.shape) for j in ids
        ]
        block = [[columns[j][base + i : base + i + 1] for j in ids] for i in ids]
        lines = [matrix[base + i : base + i + 1] for i in ids]
        for i in ids:
            scale = 1.0 / block[i][i]
            lines[i] = lines[i] * scale
            for j in range(i + 1, step):
                block[i][j] = block[i][j] * scale
            for other in ids:
                if other == i:
                    continue
                factor = block[other][i]
                lines[other] = lines[other] - factor * lines[i]
                for j in range(i + 1, step):
                    block[other][j] = block[other][j] - factor * block[i][j]
        for j in ids:
            matrix = matrix - columns[j] * lines[j]
        for j in ids:
            matrix = jnp.where(row_id == base + j, lines[j], matrix)
    return matrix


def local(states, adj_weight, adj_index, partner):
    local_cols, vertices = states.shape
    blocks, _, length, _ = adj_weight.shape
    row_devices, col_devices = lax.axis_size("rows"), lax.axis_size("cols")
    total_cols = local_cols * col_devices
    margin = blocks // 2
    width = margin * length
    rows = -(-local_cols // 16) * 16
    packed_rows = total_cols // 2
    field_shape = (2 * blocks, PARTS * rows, length)
    field = pltpu.VMEM(field_shape, jnp.bfloat16)
    full, edge, line = (rows, vertices), (rows, width), (1, vertices)
    slots = (2 * row_devices, rows, length)

    def halves(parity):
        return (
            half(parity, vertices, width, length),
            half(1 - parity, vertices, width, length),
        )

    def place(out, mate, value):
        owner, position = split(mate, blocks)
        side = lax.bitwise_and(owner, 1)
        beside = owner + 2 * side - 1
        high = lax.select(position >= margin, 1, 0)
        wanted = (high == side) & (beside >= 0) & (beside < row_devices)
        out[2 * owner] = value
        out[lax.select(wanted, 2 * beside + 1, 2 * owner)] = value

    def ones_body(ones):
        ones[...] = jnp.ones(ones.shape, ones.dtype)

    def degree_body(ones, weight, index, mates, degree, degrees):
        def one(block):
            total = None
            for k in range(weight.shape[1]):
                term = lax.dot_general(
                    ones[...],
                    weight[block, k],
                    (((1,), (1,)), ((), ())),
                    preferred_element_type=F32,
                )
                total = term if total is None else total + term
            degree[:, lanes(block, length)] = total[:1]
            degrees[pl.ds(block, 1), :] = total[:1]

        each(blocks, one)

    def image_body(index, mates, weight, degree, outer_states, inner_states, states, *refs):
        image, sent, scaled, outer, inner, spread = refs
        parity = parity_of(index)
        at_own_outer, at_own_inner = halves(parity)
        fill_extended(
            spread,
            parity,
            padded(outer_states[:, at_own_inner], rows),
            padded(states[...], rows),
            padded(inner_states[:, at_own_outer], rows),
            length,
        )

        def one(block):
            value = folded(neighbours(index, weight, spread, block), rows)
            at = lanes(block, length)
            image[:, at] = value
            scaled[:, at] = value / degree[:, at]

        each(blocks, one)
        sent[...] = image[:local_cols, :]
        inner[...] = scaled[:, at_own_inner]
        outer[:, :width] = scaled[:, at_own_outer]
        lane = lax.broadcasted_iota(jnp.int32, (rows, length), 1)
        listed = jnp.zeros((rows, length), jnp.int32)
        for block in range(blocks):
            listed = jnp.where(lane == block, mates[block], listed)
        outer[:, width:] = listed.astype(F32)

    def products_body(*refs):
        peers, (image, degree, degrees, shared, wide) = refs[:col_devices], refs[col_devices:]
        everyone = jnp.concatenate([peer[...] for peer in peers], axis=0)
        other = jnp.concatenate([everyone * degree[...], image[...]], axis=0)
        wide[...] = jnp.zeros(wide.shape, F32)
        wide[:, : total_cols + rows] = lax.dot_general(
            everyone,
            other,
            (((1,), (1,)), ((), ())),
            precision=EXACT,
            preferred_element_type=F32,
        )
        packed = wide[:packed_rows, :] + pltpu.roll(wide[packed_rows:, :], length // 2, 1)
        for device in range(row_devices):
            shared[device, :packed_rows, :] = packed
            shared[device, packed_rows:, :] = degrees[...]

    def solve_body(shared, ritz):
        total = shared[0, :packed_rows, :]
        for device in range(1, row_devices):
            total = total + shared[device, :packed_rows, :]
        total = jnp.concatenate([total, pltpu.roll(total, length // 2, 1)], axis=0)
        ritz[...] = jnp.transpose(solved(total, total_cols))[total_cols : total_cols + rows]

    def remain_body(index, mates, weight, outer, inner, shared, ritz, *refs):
        peers, refs = refs[:col_devices], refs[col_devices:]
        images, refs = refs[:col_devices], refs[col_devices:]
        own_image, scaled, degree, *refs = refs
        out, remain, residual, presmooth, pair_degree, beside, spread_field = refs
        parity = parity_of(index)
        fill_extended(spread_field, parity, outer[:, :width], scaled[...], inner[...], length)

        def offset(block):
            at = lanes(block, length)
            value = folded(neighbours(index, weight, spread_field, block), rows)
            remain[:, at] = KEEP * own_image[:, at] + DAMPING * value

        each(blocks, offset)
        everyone = jnp.concatenate([peer[...] for peer in peers], axis=0)
        spread = jnp.concatenate([image[...] for image in images], axis=0)
        mixed = jnp.dot(ritz[...], everyone, precision=EXACT, preferred_element_type=F32)
        mixed_image = jnp.dot(ritz[...], spread, precision=EXACT, preferred_element_type=F32)
        weighted = degree[...] * mixed
        residual[...] = weighted - own_image[...]
        presmooth[...] = DAMPING * (mixed - scaled[...])
        remain[...] = KEEP * weighted + DAMPING * mixed_image - remain[...]

        def one(block):
            at = lanes(block, length)
            place(out, mates[block], remain[:, at])
            owner, position = split(mates[block], blocks)
            pair_degree[:, at] = degree[:, at] + shared[owner, pl.ds(packed_rows + position, 1), :]

        each(blocks, one)
        at_outer, _ = halves(parity)
        beside[:, :width] = remain[:, at_outer]
        beside[:, width:] = jnp.zeros((rows, length), F32)
        shared_degree = pair_degree[:, at_outer]
        for block in range(margin):
            beside[block : block + 1, width:] = shared_degree[:, block * length : (block + 1) * length]

    def beside_slot(index, outer_mates, block):
        return split(outer_mates[(1 - parity_of(index)) * margin + block], blocks)[0]

    def coarse_body(
        index, mates, outer_mates, arrived, beside, remain, pair_degree, coarse, fix, further, inner
    ):
        def one(block):
            at = lanes(block, length)
            value = remain[:, at] + arrived[2 * split(mates[block], blocks)[0]]
            coarse[:, at] = value
            fix[:, at] = DAMPING * value / pair_degree[:, at]

        def other(block):
            at = lanes(block, length)
            source = beside_slot(index, outer_mates, block)
            value = beside[:, at] + arrived[2 * source + 1]
            further[:rows, at] = DAMPING * value / beside[pl.ds(block, 1), width:]
            further[rows:, at] = value

        each(blocks, one)
        each(margin, other)
        inner[...] = fix[:, halves(parity_of(index))[1]]

    def product_body(
        index, mates, weight, further, inner, fix, degree, presmooth, pair_degree, *refs
    ):
        out, product, outer, spread = refs
        fill_extended(spread, parity_of(index), further[:rows, :], fix[...], inner[...], length)

        def one(block):
            at = lanes(block, length)
            value = degree[:, at] * fix[:, at] - folded(neighbours(index, weight, spread, block), rows)
            product[:, at] = value

        each(blocks, one)
        each(blocks, lambda block: place(out, mates[block], product[:, lanes(block, length)]))
        at_outer, _ = halves(parity_of(index))
        step = DAMPING * product[:, at_outer] / pair_degree[:, at_outer]
        outer[...] = presmooth[:, at_outer] - step

    def fix_body(index, mates, outer_mates, arrived, partial, beside, further, *refs):
        product, coarse, fix, pair_degree, presmooth, second, outer, inner = refs

        def one(block):
            at = lanes(block, length)
            image = product[:, at] + arrived[2 * split(mates[block], blocks)[0]]
            step = DAMPING * (coarse[:, at] - image) / pair_degree[:, at]
            second[:, at] = presmooth[:, at] + (fix[:, at] + step)

        def other(block):
            at = lanes(block, length)
            source = beside_slot(index, outer_mates, block)
            image = further[rows:, at] - arrived[2 * source + 1]
            step = DAMPING * image / beside[pl.ds(block, 1), width:]
            outer[:, at] = partial[:, at] + (further[:rows, at] + step)

        each(blocks, one)
        each(margin, other)
        inner[...] = second[:, halves(parity_of(index))[1]]

    def smooth_body(
        index, weight, outer, inner, second, residual, degree, smooth, squares, spread
    ):
        fill_extended(spread, parity_of(index), outer[...], second[...], inner[...], length)

        def one(block):
            at = lanes(block, length)
            value, here = second[:, at], degree[:, at]
            image = here * value - folded(neighbours(index, weight, spread, block), rows)
            smooth[:, at] = value + DAMPING * (residual[:, at] - image) / here

        each(blocks, one)
        value = smooth[...]
        total = jnp.broadcast_to(jnp.sum(value * value, axis=1, keepdims=True), (rows, length))
        lane = lax.broadcasted_iota(jnp.int32, (rows // 2, length), 1)
        packed = jnp.where(lane < length // 2, total[: rows // 2], total[rows // 2 :])
        for device in range(row_devices):
            squares[device] = packed

    def scale_body(squares, smooth, correction):
        total = squares[0]
        for device in range(1, row_devices):
            total = total + squares[device]
        total = jnp.concatenate([total, pltpu.roll(total, length // 2, 1)], axis=0)
        norm = jnp.sqrt(total[:local_cols, :1] / (vertices * row_devices) + EPSILON)
        correction[...] = smooth[:local_cols, :] / norm

    adj_index = adj_index.T
    outer = across_outer(states, "rows")
    inner = across_inner(states, "rows")
    peers = exchanged(states, "cols")
    ones_shape = jax.ShapeDtypeStruct((16, length), jnp.bfloat16)
    (ones,) = kernel_call(ones_body, [ones_shape], [], [], cost=20_000_000_000)
    degree, degrees = kernel_call(
        degree_body, [line, (blocks, length)], [], [ones, adj_weight, adj_index, partner]
    )
    image, sent, scaled, outer, inner = kernel_call(
        image_body,
        [full, (local_cols, vertices), full, (rows, width + length), edge],
        [adj_index, partner],
        [adj_weight, degree, outer, inner, states],
        [field],
    )
    (shared,) = kernel_call(
        products_body,
        [(row_devices, packed_rows + blocks, length)],
        [],
        [*peers, image, degree, degrees],
        [pltpu.VMEM((total_cols, length), F32)],
    )
    shared = swapped(shared, "rows")
    outer = across_outer(outer, "rows")
    inner = across_inner(inner, "rows")
    images = exchanged(sent, "cols")
    outer_mates = outer[0, width : width + blocks].astype(jnp.int32)
    (ritz,) = kernel_call(solve_body, [(rows, total_cols)], [], [shared])
    out, remain, residual, presmooth, pair_degree, beside = kernel_call(
        remain_body,
        [slots, full, full, full, line, (rows, width + length)],
        [adj_index, partner],
        [adj_weight, outer, inner, shared, ritz, *peers, *images, image, scaled, degree],
        [field],
    )
    arrived = swapped(out, "rows")
    beside = across_outer(beside, "rows")
    coarse, fix, further, inner = kernel_call(
        coarse_body,
        [full, full, (2 * rows, width), edge],
        [adj_index, partner, outer_mates],
        [arrived, beside, remain, pair_degree],
    )
    inner = across_inner(inner, "rows")
    out, product, outer = kernel_call(
        product_body,
        [slots, full, edge],
        [adj_index, partner],
        [adj_weight, further, inner, fix, degree, presmooth, pair_degree],
        [field],
    )
    arrived = swapped(out, "rows")
    outer = across_outer(outer, "rows")
    second, outer, inner = kernel_call(
        fix_body,
        [full, edge, edge],
        [adj_index, partner, outer_mates],
        [arrived, outer, beside, further, product, coarse, fix, pair_degree, presmooth],
    )
    inner = across_inner(inner, "rows")
    smooth, squares = kernel_call(
        smooth_body,
        [full, (row_devices, rows // 2, length)],
        [adj_index],
        [adj_weight, outer, inner, second, residual, degree],
        [field],
    )
    squares = swapped(squares, "rows")
    (correction,) = kernel_call(scale_body, [states.shape], [], [squares, smooth])
    return correction


def solution(mesh):
    return jax.shard_map(
        local,
        mesh=mesh,
        in_specs=(P("cols", "rows"), P("rows", None, None, None), P("rows", None), P("rows")),
        out_specs=P("cols", "rows"),
        check_vma=False,
    )
```

```python
import jax
import jax.numpy as jnp
from jax import lax
from jax.experimental import pallas as pl
from jax.experimental.pallas import tpu as pltpu
from jax.sharding import PartitionSpec as P

DAMPING = 2.0 / 3.0
KEEP = 1.0 - DAMPING
EPSILON = 1e-06
EXACT = lax.Precision.HIGHEST
PARTS = 3
VMEM_GRANT = 16 * 1024 * 1024
F32 = jnp.float32
IN_VMEM = pl.BlockSpec(memory_space=pltpu.VMEM)
IN_SMEM = pl.BlockSpec(memory_space=pltpu.SMEM)


def kernel_call(body, outs, scalars, arrays, scratch=(), cost=2_000_000):
    return pl.pallas_call(
        body,
        out_shape=[
            out if isinstance(out, jax.ShapeDtypeStruct) else jax.ShapeDtypeStruct(out, F32)
            for out in outs
        ],
        in_specs=[IN_SMEM] * len(scalars) + [IN_VMEM] * len(arrays),
        out_specs=[IN_VMEM] * len(outs),
        scratch_shapes=list(scratch),
        compiler_params=pltpu.CompilerParams(vmem_limit_bytes=VMEM_GRANT),
        cost_estimate=pl.CostEstimate(flops=cost, bytes_accessed=cost, transcendentals=0),
    )(*scalars, *arrays)


def exchanged(value, axis):
    peers = lax.axis_size(axis)
    return [value] + [
        lax.ppermute(value, axis, [(i, i ^ mask) for i in range(peers)]) for mask in range(1, peers)
    ]


def swapped(value, axis):
    return lax.all_to_all(value, axis, split_axis=0, concat_axis=0, tiled=True)


def across_outer(value, axis):
    peers = lax.axis_size(axis)
    up = [(i, i + 1) for i in range(1, peers - 1, 2)]
    return lax.ppermute(value, axis, up + [(j, i) for i, j in up])


def across_inner(value, axis):
    return lax.ppermute(value, axis, [(i, i ^ 1) for i in range(lax.axis_size(axis))])


def each(count, body):
    if count <= 16:
        for step in range(count):
            body(step)
    else:
        lax.fori_loop(0, count, lambda step, carry: (body(step), carry)[1], 0)


def lanes(block, length):
    start = block * length
    return pl.ds(start if isinstance(block, int) else pl.multiple_of(start, length), length)


def padded(value, rows):
    if value.shape[0] == rows:
        return value
    return jnp.concatenate([value, jnp.zeros((rows - value.shape[0], value.shape[1]), F32)], axis=0)


def in_parts(value):
    pieces = []
    for _ in range(PARTS):
        piece = value.astype(jnp.bfloat16)
        pieces.append(piece)
        value = value - piece.astype(F32)
    return jnp.concatenate(pieces, axis=0)


def fill(field, base, value, length):
    split = in_parts(value)
    for block in range(value.shape[1] // length):
        field[base + block, : split.shape[0], :] = split[:, block * length : (block + 1) * length]


def split(block, blocks):
    if blocks & (blocks - 1):
        return lax.div(block, blocks), lax.rem(block, blocks)
    bits = blocks.bit_length() - 1
    return lax.shift_right_logical(block, bits), lax.bitwise_and(block, blocks - 1)


def parity_of(index):
    return lax.bitwise_and(split(index[0, 0], index.shape[1])[0], 1)


def half(parity, vertices, width, length):
    return pl.ds(pl.multiple_of(parity * (vertices - width), length), width)


def fill_extended(field, parity, outer, own, inner, length):
    margin, blocks = outer.shape[1] // length, own.shape[1] // length
    fill(field, parity * (margin + blocks), outer, length)
    fill(field, margin, own, length)
    fill(field, (1 - parity) * (margin + blocks), inner, length)


def neighbours(index, weight, field, block):
    shift = index.shape[1] // 2 - index[0, 0]
    total = None
    for k in range(index.shape[0]):
        term = lax.dot_general(
            field[index[k, block] + shift],
            weight[block, k],
            (((1,), (1,)), ((), ())),
            preferred_element_type=F32,
        )
        total = term if total is None else total + term
    return total


def folded(total, rows):
    return total[:rows] + total[rows : 2 * rows] + total[2 * rows : PARTS * rows]


def solved(matrix, size):
    row_id = lax.broadcasted_iota(jnp.int32, matrix.shape, 0)
    step = 8 if size % 8 == 0 else 1
    for base in range(0, size, step):
        ids = range(step)
        columns = [
            jnp.broadcast_to(matrix[:, base + j : base + j + 1], matrix.shape) for j in ids
        ]
        block = [[columns[j][base + i : base + i + 1] for j in ids] for i in ids]
        lines = [matrix[base + i : base + i + 1] for i in ids]
        for i in ids:
            scale = 1.0 / block[i][i]
            lines[i] = lines[i] * scale
            for j in range(i + 1, step):
                block[i][j] = block[i][j] * scale
            for other in ids:
                if other == i:
                    continue
                factor = block[other][i]
                lines[other] = lines[other] - factor * lines[i]
                for j in range(i + 1, step):
                    block[other][j] = block[other][j] - factor * block[i][j]
        for j in ids:
            matrix = matrix - columns[j] * lines[j]
        for j in ids:
            matrix = jnp.where(row_id == base + j, lines[j], matrix)
    return matrix


def local(states, adj_weight, adj_index, partner):
    local_cols, vertices = states.shape
    blocks, _, length, _ = adj_weight.shape
    row_devices, col_devices = lax.axis_size("rows"), lax.axis_size("cols")
    total_cols = local_cols * col_devices
    margin = blocks // 2
    width = margin * length
    rows = -(-local_cols // 16) * 16
    packed_rows = total_cols // 2
    field_shape = (2 * blocks, PARTS * rows, length)
    field = pltpu.VMEM(field_shape, jnp.bfloat16)
    full, edge, line = (rows, vertices), (rows, width), (1, vertices)
    slots = (2 * row_devices, rows, length)

    def halves(parity):
        return (
            half(parity, vertices, width, length),
            half(1 - parity, vertices, width, length),
        )

    def place(out, mate, value):
        owner, position = split(mate, blocks)
        side = lax.bitwise_and(owner, 1)
        beside = owner + 2 * side - 1
        high = lax.select(position >= margin, 1, 0)
        wanted = (high == side) & (beside >= 0) & (beside < row_devices)
        out[2 * owner] = value
        out[lax.select(wanted, 2 * beside + 1, 2 * owner)] = value

    def ones_body(ones):
        ones[...] = jnp.ones(ones.shape, ones.dtype)

    def degree_body(ones, weight, index, mates, degree, degrees):
        def one(block):
            total = None
            for k in range(weight.shape[1]):
                term = lax.dot_general(
                    ones[...],
                    weight[block, k],
                    (((1,), (1,)), ((), ())),
                    preferred_element_type=F32,
                )
                total = term if total is None else total + term
            degree[:, lanes(block, length)] = total[:1]
            degrees[pl.ds(block, 1), :] = total[:1]

        each(blocks, one)

    def image_body(index, mates, weight, degree, outer_states, inner_states, states, *refs):
        image, sent, scaled, outer, inner, spread = refs
        parity = parity_of(index)
        at_own_outer, at_own_inner = halves(parity)
        fill_extended(
            spread,
            parity,
            padded(outer_states[:, at_own_inner], rows),
            padded(states[...], rows),
            padded(inner_states[:, at_own_outer], rows),
            length,
        )

        def one(block):
            value = folded(neighbours(index, weight, spread, block), rows)
            at = lanes(block, length)
            image[:, at] = value
            scaled[:, at] = value / degree[:, at]

        each(blocks, one)
        sent[...] = image[:local_cols, :]
        inner[...] = scaled[:, at_own_inner]
        outer[:, :width] = scaled[:, at_own_outer]
        lane = lax.broadcasted_iota(jnp.int32, (rows, length), 1)
        listed = jnp.zeros((rows, length), jnp.int32)
        for block in range(blocks):
            listed = jnp.where(lane == block, mates[block], listed)
        outer[:, width:] = listed.astype(F32)

    def products_body(*refs):
        peers, (image, degree, degrees, shared, wide) = refs[:col_devices], refs[col_devices:]
        everyone = jnp.concatenate([peer[...] for peer in peers], axis=0)
        other = jnp.concatenate([everyone * degree[...], image[...]], axis=0)
        wide[...] = jnp.zeros(wide.shape, F32)
        wide[:, : total_cols + rows] = lax.dot_general(
            everyone,
            other,
            (((1,), (1,)), ((), ())),
            precision=EXACT,
            preferred_element_type=F32,
        )
        packed = wide[:packed_rows, :] + pltpu.roll(wide[packed_rows:, :], length // 2, 1)
        for device in range(row_devices):
            shared[device, :packed_rows, :] = packed
            shared[device, packed_rows:, :] = degrees[...]

    def solve_body(shared, ritz):
        total = shared[0, :packed_rows, :]
        for device in range(1, row_devices):
            total = total + shared[device, :packed_rows, :]
        total = jnp.concatenate([total, pltpu.roll(total, length // 2, 1)], axis=0)
        ritz[...] = jnp.transpose(solved(total, total_cols))[total_cols : total_cols + rows]

    def remain_body(index, mates, weight, outer, inner, shared, ritz, *refs):
        peers, refs = refs[:col_devices], refs[col_devices:]
        images, refs = refs[:col_devices], refs[col_devices:]
        own_image, scaled, degree, *refs = refs
        out, remain, residual, presmooth, pair_degree, beside, spread_field = refs
        parity = parity_of(index)
        fill_extended(spread_field, parity, outer[:, :width], scaled[...], inner[...], length)

        def offset(block):
            at = lanes(block, length)
            value = folded(neighbours(index, weight, spread_field, block), rows)
            remain[:, at] = KEEP * own_image[:, at] + DAMPING * value

        each(blocks, offset)
        everyone = jnp.concatenate([peer[...] for peer in peers], axis=0)
        spread = jnp.concatenate([image[...] for image in images], axis=0)
        mixed = jnp.dot(ritz[...], everyone, precision=EXACT, preferred_element_type=F32)
        mixed_image = jnp.dot(ritz[...], spread, precision=EXACT, preferred_element_type=F32)
        weighted = degree[...] * mixed
        residual[...] = weighted - own_image[...]
        presmooth[...] = DAMPING * (mixed - scaled[...])
        remain[...] = KEEP * weighted + DAMPING * mixed_image - remain[...]

        def one(block):
            at = lanes(block, length)
            place(out, mates[block], remain[:, at])
            owner, position = split(mates[block], blocks)
            pair_degree[:, at] = degree[:, at] + shared[owner, pl.ds(packed_rows + position, 1), :]

        each(blocks, one)
        at_outer, _ = halves(parity)
        beside[:, :width] = remain[:, at_outer]
        beside[:, width:] = jnp.zeros((rows, length), F32)
        shared_degree = pair_degree[:, at_outer]
        for block in range(margin):
            beside[block : block + 1, width:] = shared_degree[:, block * length : (block + 1) * length]

    def beside_slot(index, outer_mates, block):
        return split(outer_mates[(1 - parity_of(index)) * margin + block], blocks)[0]

    def coarse_body(
        index, mates, outer_mates, arrived, beside, remain, pair_degree, coarse, fix, further, inner
    ):
        def one(block):
            at = lanes(block, length)
            value = remain[:, at] + arrived[2 * split(mates[block], blocks)[0]]
            coarse[:, at] = value
            fix[:, at] = DAMPING * value / pair_degree[:, at]

        def other(block):
            at = lanes(block, length)
            source = beside_slot(index, outer_mates, block)
            value = beside[:, at] + arrived[2 * source + 1]
            further[:rows, at] = DAMPING * value / beside[pl.ds(block, 1), width:]
            further[rows:, at] = value

        each(blocks, one)
        each(margin, other)
        inner[...] = fix[:, halves(parity_of(index))[1]]

    def product_body(
        index, mates, weight, further, inner, fix, degree, presmooth, pair_degree, *refs
    ):
        out, product, outer, spread = refs
        fill_extended(spread, parity_of(index), further[:rows, :], fix[...], inner[...], length)

        def one(block):
            at = lanes(block, length)
            value = degree[:, at] * fix[:, at] - folded(neighbours(index, weight, spread, block), rows)
            product[:, at] = value

        each(blocks, one)
        each(blocks, lambda block: place(out, mates[block], product[:, lanes(block, length)]))
        at_outer, _ = halves(parity_of(index))
        step = DAMPING * product[:, at_outer] / pair_degree[:, at_outer]
        outer[...] = presmooth[:, at_outer] - step

    def fix_body(index, mates, outer_mates, arrived, partial, beside, further, *refs):
        product, coarse, fix, pair_degree, presmooth, second, outer, inner = refs

        def one(block):
            at = lanes(block, length)
            image = product[:, at] + arrived[2 * split(mates[block], blocks)[0]]
            step = DAMPING * (coarse[:, at] - image) / pair_degree[:, at]
            second[:, at] = presmooth[:, at] + (fix[:, at] + step)

        def other(block):
            at = lanes(block, length)
            source = beside_slot(index, outer_mates, block)
            image = further[rows:, at] - arrived[2 * source + 1]
            step = DAMPING * image / beside[pl.ds(block, 1), width:]
            outer[:, at] = partial[:, at] + (further[:rows, at] + step)

        each(blocks, one)
        each(margin, other)
        inner[...] = second[:, halves(parity_of(index))[1]]

    def diagonal():
        lane = lax.broadcasted_iota(jnp.int32, (rows, length), 1)
        return lane == lax.broadcasted_iota(jnp.int32, (rows, length), 0)

    def smooth_body(
        index, weight, outer, inner, second, residual, degree, smooth, squares, spread
    ):
        fill_extended(spread, parity_of(index), outer[...], second[...], inner[...], length)

        def one(block):
            at = lanes(block, length)
            value, here = second[:, at], degree[:, at]
            image = here * value - folded(neighbours(index, weight, spread, block), rows)
            smooth[:, at] = value + DAMPING * (residual[:, at] - image) / here

        each(blocks, one)
        value = smooth[...]
        total = jnp.broadcast_to(jnp.sum(value * value, axis=1, keepdims=True), (rows, length))
        packed = jnp.sum(jnp.where(diagonal(), total, 0.0), axis=0, keepdims=True)
        for device in range(row_devices):
            squares[device] = packed

    def scale_body(squares, smooth, correction):
        total = squares[0]
        for device in range(1, row_devices):
            total = total + squares[device]
        total = jnp.where(diagonal(), jnp.broadcast_to(total, (rows, length)), 0.0)
        total = jnp.sum(total, axis=1, keepdims=True)
        norm = jnp.sqrt(total[:local_cols] / (vertices * row_devices) + EPSILON)
        correction[...] = smooth[:local_cols, :] / norm

    adj_index = adj_index.T
    outer = across_outer(states, "rows")
    inner = across_inner(states, "rows")
    peers = exchanged(states, "cols")
    ones_shape = jax.ShapeDtypeStruct((16, length), jnp.bfloat16)
    (ones,) = kernel_call(ones_body, [ones_shape], [], [], cost=20_000_000_000)
    degree, degrees = kernel_call(
        degree_body, [line, (blocks, length)], [], [ones, adj_weight, adj_index, partner]
    )
    image, sent, scaled, outer, inner = kernel_call(
        image_body,
        [full, (local_cols, vertices), full, (rows, width + length), edge],
        [adj_index, partner],
        [adj_weight, degree, outer, inner, states],
        [field],
    )
    (shared,) = kernel_call(
        products_body,
        [(row_devices, packed_rows + blocks, length)],
        [],
        [*peers, image, degree, degrees],
        [pltpu.VMEM((total_cols, length), F32)],
    )
    shared = swapped(shared, "rows")
    outer = across_outer(outer, "rows")
    inner = across_inner(inner, "rows")
    images = exchanged(sent, "cols")
    outer_mates = outer[0, width : width + blocks].astype(jnp.int32)
    (ritz,) = kernel_call(solve_body, [(rows, total_cols)], [], [shared])
    out, remain, residual, presmooth, pair_degree, beside = kernel_call(
        remain_body,
        [slots, full, full, full, line, (rows, width + length)],
        [adj_index, partner],
        [adj_weight, outer, inner, shared, ritz, *peers, *images, image, scaled, degree],
        [field],
    )
    arrived = swapped(out, "rows")
    beside = across_outer(beside, "rows")
    coarse, fix, further, inner = kernel_call(
        coarse_body,
        [full, full, (2 * rows, width), edge],
        [adj_index, partner, outer_mates],
        [arrived, beside, remain, pair_degree],
    )
    inner = across_inner(inner, "rows")
    out, product, outer = kernel_call(
        product_body,
        [slots, full, edge],
        [adj_index, partner],
        [adj_weight, further, inner, fix, degree, presmooth, pair_degree],
        [field],
    )
    arrived = swapped(out, "rows")
    outer = across_outer(outer, "rows")
    second, outer, inner = kernel_call(
        fix_body,
        [full, edge, edge],
        [adj_index, partner, outer_mates],
        [arrived, outer, beside, further, product, coarse, fix, pair_degree, presmooth],
    )
    inner = across_inner(inner, "rows")
    smooth, squares = kernel_call(
        smooth_body,
        [full, (row_devices, 1, length)],
        [adj_index],
        [adj_weight, outer, inner, second, residual, degree],
        [field],
    )
    squares = swapped(squares, "rows")
    (correction,) = kernel_call(scale_body, [states.shape], [], [squares, smooth])
    return correction


def solution(mesh):
    return jax.shard_map(
        local,
        mesh=mesh,
        in_specs=(P("cols", "rows"), P("rows", None, None, None), P("rows", None), P("rows")),
        out_specs=P("cols", "rows"),
        check_vma=False,
    )
```

```python
import jax
import jax.numpy as jnp
from jax import lax
from jax.experimental import pallas as pl
from jax.experimental.pallas import tpu as pltpu
from jax.sharding import PartitionSpec as P

DAMPING = 2.0 / 3.0
KEEP = 1.0 - DAMPING
EPSILON = 1e-06
EXACT = lax.Precision.HIGHEST
PARTS = 3
VMEM_GRANT = 16 * 1024 * 1024
F32 = jnp.float32
IN_VMEM = pl.BlockSpec(memory_space=pltpu.VMEM)
IN_SMEM = pl.BlockSpec(memory_space=pltpu.SMEM)


def kernel_call(body, outs, scalars, arrays, scratch=(), cost=2_000_000):
    return pl.pallas_call(
        body,
        out_shape=[
            out if isinstance(out, jax.ShapeDtypeStruct) else jax.ShapeDtypeStruct(out, F32)
            for out in outs
        ],
        in_specs=[IN_SMEM] * len(scalars) + [IN_VMEM] * len(arrays),
        out_specs=[IN_VMEM] * len(outs),
        scratch_shapes=list(scratch),
        compiler_params=pltpu.CompilerParams(vmem_limit_bytes=VMEM_GRANT),
        cost_estimate=pl.CostEstimate(flops=cost, bytes_accessed=cost, transcendentals=0),
    )(*scalars, *arrays)


def exchanged(value, axis):
    peers = lax.axis_size(axis)
    return [value] + [
        lax.ppermute(value, axis, [(i, i ^ mask) for i in range(peers)]) for mask in range(1, peers)
    ]


def swapped(value, axis):
    return lax.all_to_all(value, axis, split_axis=0, concat_axis=0, tiled=True)


def across_outer(value, axis):
    peers = lax.axis_size(axis)
    up = [(i, i + 1) for i in range(1, peers - 1, 2)]
    return lax.ppermute(value, axis, up + [(j, i) for i, j in up])


def across_inner(value, axis):
    return lax.ppermute(value, axis, [(i, i ^ 1) for i in range(lax.axis_size(axis))])


def each(count, body):
    if count <= 16:
        for step in range(count):
            body(step)
    else:
        lax.fori_loop(0, count, lambda step, carry: (body(step), carry)[1], 0)


def lanes(block, length):
    start = block * length
    return pl.ds(start if isinstance(block, int) else pl.multiple_of(start, length), length)


def padded(value, rows):
    if value.shape[0] == rows:
        return value
    return jnp.concatenate([value, jnp.zeros((rows - value.shape[0], value.shape[1]), F32)], axis=0)


def in_parts(value):
    pieces = []
    for _ in range(PARTS):
        piece = value.astype(jnp.bfloat16)
        pieces.append(piece)
        value = value - piece.astype(F32)
    return jnp.concatenate(pieces, axis=0)


def fill(field, base, value, length):
    split = in_parts(value)
    for block in range(value.shape[1] // length):
        field[base + block, : split.shape[0], :] = split[:, block * length : (block + 1) * length]


def split(block, blocks):
    if blocks & (blocks - 1):
        return lax.div(block, blocks), lax.rem(block, blocks)
    bits = blocks.bit_length() - 1
    return lax.shift_right_logical(block, bits), lax.bitwise_and(block, blocks - 1)


def parity_of(index):
    return lax.bitwise_and(split(index[0, 0], index.shape[1])[0], 1)


def half(parity, vertices, width, length):
    return pl.ds(pl.multiple_of(parity * (vertices - width), length), width)


def fill_extended(field, parity, outer, own, inner, length):
    margin, blocks = outer.shape[1] // length, own.shape[1] // length
    fill(field, parity * (margin + blocks), outer, length)
    fill(field, margin, own, length)
    fill(field, (1 - parity) * (margin + blocks), inner, length)


def neighbours(index, weight, field, block):
    shift = index.shape[1] // 2 - index[0, 0]
    total = None
    for k in range(index.shape[0]):
        term = lax.dot_general(
            field[index[k, block] + shift],
            weight[block, k],
            (((1,), (1,)), ((), ())),
            preferred_element_type=F32,
        )
        total = term if total is None else total + term
    return total


def folded(total, rows):
    return total[:rows] + total[rows : 2 * rows] + total[2 * rows : PARTS * rows]


def solved(matrix, size):
    row_id = lax.broadcasted_iota(jnp.int32, matrix.shape, 0)
    step = 8 if size % 8 == 0 else 1
    for base in range(0, size, step):
        ids = range(step)
        columns = [
            jnp.broadcast_to(matrix[:, base + j : base + j + 1], matrix.shape) for j in ids
        ]
        block = [[columns[j][base + i : base + i + 1] for j in ids] for i in ids]
        lines = [matrix[base + i : base + i + 1] for i in ids]
        for i in ids:
            scale = 1.0 / block[i][i]
            lines[i] = lines[i] * scale
            for j in range(i + 1, step):
                block[i][j] = block[i][j] * scale
            for other in ids:
                if other == i:
                    continue
                factor = block[other][i]
                lines[other] = lines[other] - factor * lines[i]
                for j in range(i + 1, step):
                    block[other][j] = block[other][j] - factor * block[i][j]
        for j in ids:
            matrix = matrix - columns[j] * lines[j]
        for j in ids:
            matrix = jnp.where(row_id == base + j, lines[j], matrix)
    return matrix


def local(states, adj_weight, adj_index, partner):
    local_cols, vertices = states.shape
    blocks, _, length, _ = adj_weight.shape
    row_devices, col_devices = lax.axis_size("rows"), lax.axis_size("cols")
    total_cols = local_cols * col_devices
    margin = blocks // 2
    width = margin * length
    rows = -(-local_cols // 16) * 16
    packed_rows = total_cols // 2
    field_shape = (2 * blocks, PARTS * rows, length)
    field = pltpu.VMEM(field_shape, jnp.bfloat16)
    full, edge, line = (rows, vertices), (rows, width), (1, vertices)
    slots = (2 * row_devices, rows, length)

    def halves(parity):
        return (
            half(parity, vertices, width, length),
            half(1 - parity, vertices, width, length),
        )

    def place(out, mate, value):
        owner, position = split(mate, blocks)
        side = lax.bitwise_and(owner, 1)
        beside = owner + 2 * side - 1
        high = lax.select(position >= margin, 1, 0)
        wanted = (high == side) & (beside >= 0) & (beside < row_devices)
        out[2 * owner] = value
        out[lax.select(wanted, 2 * beside + 1, 2 * owner)] = value

    def ones_body(ones):
        ones[...] = jnp.ones(ones.shape, ones.dtype)

    def degree_body(ones, weight, index, mates, degree):
        def one(block):
            total = None
            for k in range(weight.shape[1]):
                term = lax.dot_general(
                    ones[...],
                    weight[block, k],
                    (((1,), (1,)), ((), ())),
                    preferred_element_type=F32,
                )
                total = term if total is None else total + term
            degree[:, lanes(block, length)] = total[:1]

        each(blocks, one)

    def image_body(index, mates, weight, degree, outer_states, inner_states, states, *refs):
        image, sent, scaled, outer, inner, degrees, spread = refs
        parity = parity_of(index)
        at_own_outer, at_own_inner = halves(parity)
        fill_extended(
            spread,
            parity,
            padded(outer_states[:, at_own_inner], rows),
            padded(states[...], rows),
            padded(inner_states[:, at_own_outer], rows),
            length,
        )

        def one(block):
            value = folded(neighbours(index, weight, spread, block), rows)
            at = lanes(block, length)
            image[:, at] = value
            scaled[:, at] = value / degree[:, at]

        each(blocks, one)
        for block in range(blocks):
            degrees[split(mates[block], blocks)[0]] = degree[:, lanes(block, length)]
        sent[...] = image[:local_cols, :]
        inner[...] = scaled[:, at_own_inner]
        outer[:, :width] = scaled[:, at_own_outer]
        lane = lax.broadcasted_iota(jnp.int32, (rows, length), 1)
        listed = jnp.zeros((rows, length), jnp.int32)
        for block in range(blocks):
            listed = jnp.where(lane == block, mates[block], listed)
        outer[:, width:] = listed.astype(F32)

    def products_body(*refs):
        peers, (image, degree, degrees, shared, wide, flat) = (
            refs[:col_devices],
            refs[col_devices:],
        )
        everyone = jnp.concatenate([peer[...] for peer in peers], axis=0)
        other = jnp.concatenate([everyone * degree[...], image[...]], axis=0)
        wide[...] = jnp.zeros(wide.shape, F32)
        wide[:, : total_cols + rows] = lax.dot_general(
            everyone,
            other,
            (((1,), (1,)), ((), ())),
            precision=EXACT,
            preferred_element_type=F32,
        )
        packed = wide[:packed_rows, :] + pltpu.roll(wide[packed_rows:, :], length // 2, 1)
        for row in range(packed_rows):
            flat[:, lanes(row, length)] = packed[row : row + 1]
        value = flat[...]
        for device in range(row_devices):
            shared[device, :, : packed_rows * length] = value
            shared[device, :, packed_rows * length :] = degrees[device]

    def solve_body(shared, ritz, tall):
        total = shared[0, :, : packed_rows * length]
        for device in range(1, row_devices):
            total = total + shared[device, :, : packed_rows * length]
        for row in range(packed_rows):
            tall[row : row + 1, :] = total[:, row * length : (row + 1) * length]
        total = tall[...]
        total = jnp.concatenate([total, pltpu.roll(total, length // 2, 1)], axis=0)
        ritz[...] = jnp.transpose(solved(total, total_cols))[total_cols : total_cols + rows]

    def remain_body(index, mates, weight, outer, inner, shared, ritz, *refs):
        peers, refs = refs[:col_devices], refs[col_devices:]
        images, refs = refs[:col_devices], refs[col_devices:]
        own_image, scaled, degree, *refs = refs
        out, remain, residual, presmooth, pair_degree, beside, spread_field = refs
        parity = parity_of(index)
        fill_extended(spread_field, parity, outer[:, :width], scaled[...], inner[...], length)

        def offset(block):
            at = lanes(block, length)
            value = folded(neighbours(index, weight, spread_field, block), rows)
            remain[:, at] = KEEP * own_image[:, at] + DAMPING * value

        each(blocks, offset)
        everyone = jnp.concatenate([peer[...] for peer in peers], axis=0)
        spread = jnp.concatenate([image[...] for image in images], axis=0)
        mixed = jnp.dot(ritz[...], everyone, precision=EXACT, preferred_element_type=F32)
        mixed_image = jnp.dot(ritz[...], spread, precision=EXACT, preferred_element_type=F32)
        weighted = degree[...] * mixed
        residual[...] = weighted - own_image[...]
        presmooth[...] = DAMPING * (mixed - scaled[...])
        remain[...] = KEEP * weighted + DAMPING * mixed_image - remain[...]

        def one(block):
            at = lanes(block, length)
            place(out, mates[block], remain[:, at])
            owner, _ = split(mates[block], blocks)
            pair_degree[:, at] = degree[:, at] + shared[owner, :, packed_rows * length :]

        each(blocks, one)
        at_outer, _ = halves(parity)
        beside[:, :width] = remain[:, at_outer]
        beside[:, width:] = jnp.zeros((rows, length), F32)
        shared_degree = pair_degree[:, at_outer]
        for block in range(margin):
            beside[block : block + 1, width:] = shared_degree[:, block * length : (block + 1) * length]

    def beside_slot(index, outer_mates, block):
        return split(outer_mates[(1 - parity_of(index)) * margin + block], blocks)[0]

    def coarse_body(
        index, mates, outer_mates, arrived, beside, remain, pair_degree, coarse, fix, further, inner
    ):
        def one(block):
            at = lanes(block, length)
            value = remain[:, at] + arrived[2 * split(mates[block], blocks)[0]]
            coarse[:, at] = value
            fix[:, at] = DAMPING * value / pair_degree[:, at]

        def other(block):
            at = lanes(block, length)
            source = beside_slot(index, outer_mates, block)
            value = beside[:, at] + arrived[2 * source + 1]
            further[:rows, at] = DAMPING * value / beside[pl.ds(block, 1), width:]
            further[rows:, at] = value

        each(blocks, one)
        each(margin, other)
        inner[...] = fix[:, halves(parity_of(index))[1]]

    def product_body(
        index, mates, weight, further, inner, fix, degree, presmooth, pair_degree, *refs
    ):
        out, product, outer, spread = refs
        fill_extended(spread, parity_of(index), further[:rows, :], fix[...], inner[...], length)

        def one(block):
            at = lanes(block, length)
            value = degree[:, at] * fix[:, at] - folded(neighbours(index, weight, spread, block), rows)
            product[:, at] = value

        each(blocks, one)
        each(blocks, lambda block: place(out, mates[block], product[:, lanes(block, length)]))
        at_outer, _ = halves(parity_of(index))
        step = DAMPING * product[:, at_outer] / pair_degree[:, at_outer]
        outer[...] = presmooth[:, at_outer] - step

    def fix_body(index, mates, outer_mates, arrived, partial, beside, further, *refs):
        product, coarse, fix, pair_degree, presmooth, second, outer, inner = refs

        def one(block):
            at = lanes(block, length)
            image = product[:, at] + arrived[2 * split(mates[block], blocks)[0]]
            step = DAMPING * (coarse[:, at] - image) / pair_degree[:, at]
            second[:, at] = presmooth[:, at] + (fix[:, at] + step)

        def other(block):
            at = lanes(block, length)
            source = beside_slot(index, outer_mates, block)
            image = further[rows:, at] - arrived[2 * source + 1]
            step = DAMPING * image / beside[pl.ds(block, 1), width:]
            outer[:, at] = partial[:, at] + (further[:rows, at] + step)

        each(blocks, one)
        each(margin, other)
        inner[...] = second[:, halves(parity_of(index))[1]]

    def diagonal():
        lane = lax.broadcasted_iota(jnp.int32, (rows, length), 1)
        return lane == lax.broadcasted_iota(jnp.int32, (rows, length), 0)

    def smooth_body(
        index, weight, outer, inner, second, residual, degree, smooth, squares, spread
    ):
        fill_extended(spread, parity_of(index), outer[...], second[...], inner[...], length)

        def one(block):
            at = lanes(block, length)
            value, here = second[:, at], degree[:, at]
            image = here * value - folded(neighbours(index, weight, spread, block), rows)
            smooth[:, at] = value + DAMPING * (residual[:, at] - image) / here

        each(blocks, one)
        value = smooth[...]
        total = jnp.broadcast_to(jnp.sum(value * value, axis=1, keepdims=True), (rows, length))
        packed = jnp.sum(jnp.where(diagonal(), total, 0.0), axis=0, keepdims=True)
        for device in range(row_devices):
            squares[device] = packed

    def scale_body(squares, smooth, correction):
        total = squares[0]
        for device in range(1, row_devices):
            total = total + squares[device]
        total = jnp.where(diagonal(), jnp.broadcast_to(total, (rows, length)), 0.0)
        total = jnp.sum(total, axis=1, keepdims=True)
        norm = jnp.sqrt(total[:local_cols] / (vertices * row_devices) + EPSILON)
        correction[...] = smooth[:local_cols, :] / norm

    adj_index = adj_index.T
    outer = across_outer(states, "rows")
    inner = across_inner(states, "rows")
    peers = exchanged(states, "cols")
    ones_shape = jax.ShapeDtypeStruct((16, length), jnp.bfloat16)
    (ones,) = kernel_call(ones_body, [ones_shape], [], [], cost=20_000_000_000)
    (degree,) = kernel_call(degree_body, [line], [], [ones, adj_weight, adj_index, partner])
    image, sent, scaled, outer, inner, degrees = kernel_call(
        image_body,
        [
            full,
            (local_cols, vertices),
            full,
            (rows, width + length),
            edge,
            (row_devices, 1, length),
        ],
        [adj_index, partner],
        [adj_weight, degree, outer, inner, states],
        [field],
    )
    (shared,) = kernel_call(
        products_body,
        [(row_devices, 1, (packed_rows + 1) * length)],
        [],
        [*peers, image, degree, degrees],
        [pltpu.VMEM((total_cols, length), F32), pltpu.VMEM((1, packed_rows * length), F32)],
    )
    shared = swapped(shared, "rows")
    outer = across_outer(outer, "rows")
    inner = across_inner(inner, "rows")
    images = exchanged(sent, "cols")
    outer_mates = outer[0, width : width + blocks].astype(jnp.int32)
    (ritz,) = kernel_call(
        solve_body, [(rows, total_cols)], [], [shared], [pltpu.VMEM((packed_rows, length), F32)]
    )
    out, remain, residual, presmooth, pair_degree, beside = kernel_call(
        remain_body,
        [slots, full, full, full, line, (rows, width + length)],
        [adj_index, partner],
        [adj_weight, outer, inner, shared, ritz, *peers, *images, image, scaled, degree],
        [field],
    )
    arrived = swapped(out, "rows")
    beside = across_outer(beside, "rows")
    coarse, fix, further, inner = kernel_call(
        coarse_body,
        [full, full, (2 * rows, width), edge],
        [adj_index, partner, outer_mates],
        [arrived, beside, remain, pair_degree],
    )
    inner = across_inner(inner, "rows")
    out, product, outer = kernel_call(
        product_body,
        [slots, full, edge],
        [adj_index, partner],
        [adj_weight, further, inner, fix, degree, presmooth, pair_degree],
        [field],
    )
    arrived = swapped(out, "rows")
    outer = across_outer(outer, "rows")
    second, outer, inner = kernel_call(
        fix_body,
        [full, edge, edge],
        [adj_index, partner, outer_mates],
        [arrived, outer, beside, further, product, coarse, fix, pair_degree, presmooth],
    )
    inner = across_inner(inner, "rows")
    smooth, squares = kernel_call(
        smooth_body,
        [full, (row_devices, 1, length)],
        [adj_index],
        [adj_weight, outer, inner, second, residual, degree],
        [field],
    )
    squares = swapped(squares, "rows")
    (correction,) = kernel_call(scale_body, [states.shape], [], [squares, smooth])
    return correction


def solution(mesh):
    return jax.shard_map(
        local,
        mesh=mesh,
        in_specs=(P("cols", "rows"), P("rows", None, None, None), P("rows", None), P("rows")),
        out_specs=P("cols", "rows"),
        check_vma=False,
    )
```

```python
import jax
import jax.numpy as jnp
from jax import lax
from jax.experimental import pallas as pl
from jax.experimental.pallas import tpu as pltpu
from jax.sharding import PartitionSpec as P

DAMPING = 2.0 / 3.0
KEEP = 1.0 - DAMPING
EPSILON = 1e-06
EXACT = lax.Precision.HIGHEST
PARTS = 3
VMEM_GRANT = 16 * 1024 * 1024
F32 = jnp.float32
IN_VMEM = pl.BlockSpec(memory_space=pltpu.VMEM)
IN_SMEM = pl.BlockSpec(memory_space=pltpu.SMEM)


def kernel_call(body, outs, scalars, arrays, scratch=(), cost=2_000_000):
    return pl.pallas_call(
        body,
        out_shape=[
            out if isinstance(out, jax.ShapeDtypeStruct) else jax.ShapeDtypeStruct(out, F32)
            for out in outs
        ],
        in_specs=[IN_SMEM] * len(scalars) + [IN_VMEM] * len(arrays),
        out_specs=[IN_VMEM] * len(outs),
        scratch_shapes=list(scratch),
        compiler_params=pltpu.CompilerParams(vmem_limit_bytes=VMEM_GRANT),
        cost_estimate=pl.CostEstimate(flops=cost, bytes_accessed=cost, transcendentals=0),
    )(*scalars, *arrays)


def exchanged(value, axis):
    peers = lax.axis_size(axis)
    return [value] + [
        lax.ppermute(value, axis, [(i, i ^ mask) for i in range(peers)]) for mask in range(1, peers)
    ]


def swapped(value, axis):
    return lax.all_to_all(value, axis, split_axis=0, concat_axis=0, tiled=True)


def across_outer(value, axis):
    peers = lax.axis_size(axis)
    up = [(i, i + 1) for i in range(1, peers - 1, 2)]
    return lax.ppermute(value, axis, up + [(j, i) for i, j in up])


def across_inner(value, axis):
    return lax.ppermute(value, axis, [(i, i ^ 1) for i in range(lax.axis_size(axis))])


def each(count, body):
    if count <= 16:
        for step in range(count):
            body(step)
    else:
        lax.fori_loop(0, count, lambda step, carry: (body(step), carry)[1], 0)


def lanes(block, length):
    start = block * length
    return pl.ds(start if isinstance(block, int) else pl.multiple_of(start, length), length)


def padded(value, rows):
    if value.shape[0] == rows:
        return value
    return jnp.concatenate([value, jnp.zeros((rows - value.shape[0], value.shape[1]), F32)], axis=0)


def in_parts(value):
    pieces = []
    for _ in range(PARTS):
        piece = value.astype(jnp.bfloat16)
        pieces.append(piece)
        value = value - piece.astype(F32)
    return jnp.concatenate(pieces, axis=0)


def fill(field, base, value, length):
    split = in_parts(value)
    for block in range(value.shape[1] // length):
        field[base + block, : split.shape[0], :] = split[:, block * length : (block + 1) * length]


def split(block, blocks):
    if blocks & (blocks - 1):
        return lax.div(block, blocks), lax.rem(block, blocks)
    bits = blocks.bit_length() - 1
    return lax.shift_right_logical(block, bits), lax.bitwise_and(block, blocks - 1)


def parity_of(index):
    return lax.bitwise_and(split(index[0, 0], index.shape[1])[0], 1)


def half(parity, vertices, width, length):
    return pl.ds(pl.multiple_of(parity * (vertices - width), length), width)


def fill_extended(field, parity, outer, own, inner, length):
    margin, blocks = outer.shape[1] // length, own.shape[1] // length
    fill(field, parity * (margin + blocks), outer, length)
    fill(field, margin, own, length)
    fill(field, (1 - parity) * (margin + blocks), inner, length)


def neighbours(index, weight, field, block):
    shift = index.shape[1] // 2 - index[0, 0]
    total = None
    for k in range(index.shape[0]):
        term = lax.dot_general(
            field[index[k, block] + shift],
            weight[block, k],
            (((1,), (1,)), ((), ())),
            preferred_element_type=F32,
        )
        total = term if total is None else total + term
    return total


def folded(total, rows):
    return total[:rows] + total[rows : 2 * rows] + total[2 * rows : PARTS * rows]


def solved(matrix, size):
    row_id = lax.broadcasted_iota(jnp.int32, matrix.shape, 0)
    step = 8 if size % 8 == 0 else 1
    for base in range(0, size, step):
        ids = range(step)
        columns = [
            jnp.broadcast_to(matrix[:, base + j : base + j + 1], matrix.shape) for j in ids
        ]
        block = [[columns[j][base + i : base + i + 1] for j in ids] for i in ids]
        lines = [matrix[base + i : base + i + 1] for i in ids]
        for i in ids:
            scale = 1.0 / block[i][i]
            lines[i] = lines[i] * scale
            for j in range(i + 1, step):
                block[i][j] = block[i][j] * scale
            for other in ids:
                if other == i:
                    continue
                factor = block[other][i]
                lines[other] = lines[other] - factor * lines[i]
                for j in range(i + 1, step):
                    block[other][j] = block[other][j] - factor * block[i][j]
        for j in ids:
            matrix = matrix - columns[j] * lines[j]
        for j in ids:
            matrix = jnp.where(row_id == base + j, lines[j], matrix)
    return matrix


def local(states, adj_weight, adj_index, partner):
    local_cols, vertices = states.shape
    blocks, _, length, _ = adj_weight.shape
    row_devices, col_devices = lax.axis_size("rows"), lax.axis_size("cols")
    total_cols = local_cols * col_devices
    margin = blocks // 2
    width = margin * length
    rows = -(-local_cols // 16) * 16
    packed_rows = total_cols // 2
    field_shape = (2 * blocks, PARTS * rows, length)
    field = pltpu.VMEM(field_shape, jnp.bfloat16)
    full, edge, line = (rows, vertices), (rows, width), (1, vertices)
    slots = (2 * row_devices, rows, length)

    def halves(parity):
        return (
            half(parity, vertices, width, length),
            half(1 - parity, vertices, width, length),
        )

    def place(out, mate, value):
        owner, position = split(mate, blocks)
        side = lax.bitwise_and(owner, 1)
        beside = owner + 2 * side - 1
        high = lax.select(position >= margin, 1, 0)
        wanted = (high == side) & (beside >= 0) & (beside < row_devices)
        out[2 * owner] = value
        out[lax.select(wanted, 2 * beside + 1, 2 * owner)] = value

    def ones_body(ones):
        ones[...] = jnp.ones(ones.shape, ones.dtype)

    def degree_body(ones, weight, index, mates, degree):
        def one(block):
            total = None
            for k in range(weight.shape[1]):
                term = lax.dot_general(
                    ones[...],
                    weight[block, k],
                    (((1,), (1,)), ((), ())),
                    preferred_element_type=F32,
                )
                total = term if total is None else total + term
            degree[:, lanes(block, length)] = total[:1]

        each(blocks, one)

    def image_body(index, mates, weight, degree, outer_states, inner_states, states, *refs):
        image, sent, scaled, outer, inner, degrees, spread = refs
        parity = parity_of(index)
        at_own_outer, at_own_inner = halves(parity)
        fill_extended(
            spread,
            parity,
            padded(outer_states[:, at_own_inner], rows),
            padded(states[...], rows),
            padded(inner_states[:, at_own_outer], rows),
            length,
        )

        def one(block):
            value = folded(neighbours(index, weight, spread, block), rows)
            at = lanes(block, length)
            image[:, at] = value
            scaled[:, at] = value / degree[:, at]

        each(blocks, one)
        for block in range(blocks):
            degrees[split(mates[block], blocks)[0]] = degree[:, lanes(block, length)]
        sent[...] = image[:local_cols, :]
        inner[...] = scaled[:, at_own_inner]
        outer[:, :width] = scaled[:, at_own_outer]
        lane = lax.broadcasted_iota(jnp.int32, (rows, length), 1)
        listed = jnp.zeros((rows, length), jnp.int32)
        for block in range(blocks):
            listed = jnp.where(lane == block, mates[block], listed)
        outer[:, width:] = listed.astype(F32)

    def products_body(*refs):
        peers, (image, degree, degrees, shared, wide, flat) = (
            refs[:col_devices],
            refs[col_devices:],
        )
        everyone = jnp.concatenate([peer[...] for peer in peers], axis=0)
        other = jnp.concatenate([everyone * degree[...], image[...]], axis=0)
        wide[...] = jnp.zeros(wide.shape, F32)
        wide[:, : total_cols + rows] = lax.dot_general(
            everyone,
            other,
            (((1,), (1,)), ((), ())),
            precision=EXACT,
            preferred_element_type=F32,
        )
        packed = wide[:packed_rows, :] + pltpu.roll(wide[packed_rows:, :], length // 2, 1)
        for row in range(packed_rows):
            flat[:, lanes(row, length)] = packed[row : row + 1]
        value = flat[...]
        for device in range(row_devices):
            shared[device, :, : packed_rows * length] = value
            shared[device, :, packed_rows * length :] = degrees[device]

    def solve_body(shared, ritz, tall):
        total = shared[0, :, : packed_rows * length]
        for device in range(1, row_devices):
            total = total + shared[device, :, : packed_rows * length]
        for row in range(packed_rows):
            tall[row : row + 1, :] = total[:, row * length : (row + 1) * length]
        total = tall[...]
        total = jnp.concatenate([total, pltpu.roll(total, length // 2, 1)], axis=0)
        ritz[...] = jnp.transpose(solved(total, total_cols))[total_cols : total_cols + rows]

    def remain_body(index, mates, weight, outer, inner, shared, ritz, *refs):
        peers, refs = refs[:col_devices], refs[col_devices:]
        images, refs = refs[:col_devices], refs[col_devices:]
        own_image, scaled, degree, *refs = refs
        out, remain, residual, presmooth, pair_degree, beside, spread_field = refs
        parity = parity_of(index)
        fill_extended(spread_field, parity, outer[:, :width], scaled[...], inner[...], length)

        def offset(block):
            at = lanes(block, length)
            value = folded(neighbours(index, weight, spread_field, block), rows)
            remain[:, at] = KEEP * own_image[:, at] + DAMPING * value

        each(blocks, offset)
        everyone = jnp.concatenate([peer[...] for peer in peers], axis=0)
        spread = jnp.concatenate([image[...] for image in images], axis=0)
        mixed = jnp.dot(ritz[...], everyone, precision=EXACT, preferred_element_type=F32)
        mixed_image = jnp.dot(ritz[...], spread, precision=EXACT, preferred_element_type=F32)
        weighted = degree[...] * mixed
        residual[...] = weighted - own_image[...]
        presmooth[...] = DAMPING * (mixed - scaled[...])
        remain[...] = KEEP * weighted + DAMPING * mixed_image - remain[...]

        def one(block):
            at = lanes(block, length)
            place(out, mates[block], remain[:, at])
            owner, _ = split(mates[block], blocks)
            pair_degree[:, at] = degree[:, at] + shared[owner, :, packed_rows * length :]

        each(blocks, one)
        at_outer, _ = halves(parity)
        beside[:, :width] = remain[:, at_outer]
        beside[:, width:] = jnp.zeros((rows, length), F32)
        shared_degree = pair_degree[:, at_outer]
        for block in range(margin):
            beside[block : block + 1, width:] = shared_degree[:, block * length : (block + 1) * length]

    def masks_body(index, mates, outer_mates, masks):
        parity = parity_of(index)
        source = lax.broadcasted_iota(jnp.int32, (row_devices, length), 0)
        for block in range(blocks + margin):
            if block < blocks:
                mate = mates[block]
            else:
                mate = outer_mates[(1 - parity) * margin + block - blocks]
            here = source == split(mate, blocks)[0]
            masks[block * row_devices : (block + 1) * row_devices, :] = jnp.where(here, 1.0, 0.0)
        masks[(blocks + margin) * row_devices :, :] = jnp.full((8, length), parity, F32)

    def chosen(masks, arrived, block, slot):
        value = arrived[slot]
        for device in range(1, row_devices):
            row = block * row_devices + device
            here = jnp.broadcast_to(masks[row : row + 1, :], (rows, length)) > 0.5
            value = jnp.where(here, arrived[2 * device + slot], value)
        return value

    def inner_half(masks, value):
        row = (blocks + margin) * row_devices
        odd = jnp.broadcast_to(masks[row : row + 1, :1], (rows, width)) > 0.5
        return jnp.where(odd, value[:, :width], value[:, vertices - width :])

    def coarse_body(masks, arrived, beside, remain, pair_degree, coarse, fix, further, inner):
        def one(block):
            at = lanes(block, length)
            value = remain[:, at] + chosen(masks, arrived, block, 0)
            coarse[:, at] = value
            fix[:, at] = DAMPING * value / pair_degree[:, at]

        def other(block):
            at = lanes(block, length)
            value = beside[:, at] + chosen(masks, arrived, blocks + block, 1)
            further[:rows, at] = DAMPING * value / beside[block : block + 1, width:]
            further[rows:, at] = value

        for block in range(blocks):
            one(block)
        for block in range(margin):
            other(block)
        inner[...] = inner_half(masks, fix[...])

    def product_body(
        index, mates, weight, further, inner, fix, degree, presmooth, pair_degree, *refs
    ):
        out, product, outer, spread = refs
        fill_extended(spread, parity_of(index), further[:rows, :], fix[...], inner[...], length)

        def one(block):
            at = lanes(block, length)
            value = degree[:, at] * fix[:, at] - folded(neighbours(index, weight, spread, block), rows)
            product[:, at] = value

        each(blocks, one)
        each(blocks, lambda block: place(out, mates[block], product[:, lanes(block, length)]))
        at_outer, _ = halves(parity_of(index))
        step = DAMPING * product[:, at_outer] / pair_degree[:, at_outer]
        outer[...] = presmooth[:, at_outer] - step

    def fix_body(masks, arrived, partial, beside, further, *refs):
        product, coarse, fix, pair_degree, presmooth, second, outer, inner = refs

        def one(block):
            at = lanes(block, length)
            image = product[:, at] + chosen(masks, arrived, block, 0)
            step = DAMPING * (coarse[:, at] - image) / pair_degree[:, at]
            second[:, at] = presmooth[:, at] + (fix[:, at] + step)

        def other(block):
            at = lanes(block, length)
            image = further[rows:, at] - chosen(masks, arrived, blocks + block, 1)
            step = DAMPING * image / beside[block : block + 1, width:]
            outer[:, at] = partial[:, at] + (further[:rows, at] + step)

        for block in range(blocks):
            one(block)
        for block in range(margin):
            other(block)
        inner[...] = inner_half(masks, second[...])

    def diagonal():
        lane = lax.broadcasted_iota(jnp.int32, (rows, length), 1)
        return lane == lax.broadcasted_iota(jnp.int32, (rows, length), 0)

    def smooth_body(
        index, weight, outer, inner, second, residual, degree, smooth, squares, spread
    ):
        fill_extended(spread, parity_of(index), outer[...], second[...], inner[...], length)

        def one(block):
            at = lanes(block, length)
            value, here = second[:, at], degree[:, at]
            image = here * value - folded(neighbours(index, weight, spread, block), rows)
            smooth[:, at] = value + DAMPING * (residual[:, at] - image) / here

        each(blocks, one)
        value = smooth[...]
        total = jnp.broadcast_to(jnp.sum(value * value, axis=1, keepdims=True), (rows, length))
        packed = jnp.sum(jnp.where(diagonal(), total, 0.0), axis=0, keepdims=True)
        for device in range(row_devices):
            squares[device] = packed

    def scale_body(squares, smooth, correction):
        total = squares[0]
        for device in range(1, row_devices):
            total = total + squares[device]
        total = jnp.where(diagonal(), jnp.broadcast_to(total, (rows, length)), 0.0)
        total = jnp.sum(total, axis=1, keepdims=True)
        norm = jnp.sqrt(total[:local_cols] / (vertices * row_devices) + EPSILON)
        correction[...] = smooth[:local_cols, :] / norm

    adj_index = adj_index.T
    outer = across_outer(states, "rows")
    inner = across_inner(states, "rows")
    peers = exchanged(states, "cols")
    ones_shape = jax.ShapeDtypeStruct((16, length), jnp.bfloat16)
    (ones,) = kernel_call(ones_body, [ones_shape], [], [], cost=20_000_000_000)
    (degree,) = kernel_call(degree_body, [line], [], [ones, adj_weight, adj_index, partner])
    image, sent, scaled, outer, inner, degrees = kernel_call(
        image_body,
        [
            full,
            (local_cols, vertices),
            full,
            (rows, width + length),
            edge,
            (row_devices, 1, length),
        ],
        [adj_index, partner],
        [adj_weight, degree, outer, inner, states],
        [field],
    )
    (shared,) = kernel_call(
        products_body,
        [(row_devices, 1, (packed_rows + 1) * length)],
        [],
        [*peers, image, degree, degrees],
        [pltpu.VMEM((total_cols, length), F32), pltpu.VMEM((1, packed_rows * length), F32)],
    )
    shared = swapped(shared, "rows")
    outer = across_outer(outer, "rows")
    inner = across_inner(inner, "rows")
    images = exchanged(sent, "cols")
    outer_mates = outer[0, width : width + blocks].astype(jnp.int32)
    (ritz,) = kernel_call(
        solve_body, [(rows, total_cols)], [], [shared], [pltpu.VMEM((packed_rows, length), F32)]
    )
    out, remain, residual, presmooth, pair_degree, beside = kernel_call(
        remain_body,
        [slots, full, full, full, line, (rows, width + length)],
        [adj_index, partner],
        [adj_weight, outer, inner, shared, ritz, *peers, *images, image, scaled, degree],
        [field],
    )
    arrived = swapped(out, "rows")
    beside = across_outer(beside, "rows")
    (masks,) = kernel_call(
        masks_body,
        [((blocks + margin) * row_devices + 8, length)],
        [adj_index, partner, outer_mates],
        [],
    )
    coarse, fix, further, inner = kernel_call(
        coarse_body,
        [full, full, (2 * rows, width), edge],
        [],
        [masks, arrived, beside, remain, pair_degree],
    )
    inner = across_inner(inner, "rows")
    out, product, outer = kernel_call(
        product_body,
        [slots, full, edge],
        [adj_index, partner],
        [adj_weight, further, inner, fix, degree, presmooth, pair_degree],
        [field],
    )
    arrived = swapped(out, "rows")
    outer = across_outer(outer, "rows")
    second, outer, inner = kernel_call(
        fix_body,
        [full, edge, edge],
        [],
        [masks, arrived, outer, beside, further, product, coarse, fix, pair_degree, presmooth],
    )
    inner = across_inner(inner, "rows")
    smooth, squares = kernel_call(
        smooth_body,
        [full, (row_devices, 1, length)],
        [adj_index],
        [adj_weight, outer, inner, second, residual, degree],
        [field],
    )
    squares = swapped(squares, "rows")
    (correction,) = kernel_call(scale_body, [states.shape], [], [squares, smooth])
    return correction


def solution(mesh):
    return jax.shard_map(
        local,
        mesh=mesh,
        in_specs=(P("cols", "rows"), P("rows", None, None, None), P("rows", None), P("rows")),
        out_specs=P("cols", "rows"),
        check_vma=False,
    )
```

```python
import jax
import jax.numpy as jnp
from jax import lax
from jax.experimental import pallas as pl
from jax.experimental.pallas import tpu as pltpu
from jax.sharding import PartitionSpec as P

DAMPING = 2.0 / 3.0
KEEP = 1.0 - DAMPING
EPSILON = 1e-06
EXACT = lax.Precision.HIGHEST
PARTS = 3
VMEM_GRANT = 16 * 1024 * 1024
F32 = jnp.float32
IN_VMEM = pl.BlockSpec(memory_space=pltpu.VMEM)
IN_SMEM = pl.BlockSpec(memory_space=pltpu.SMEM)


def kernel_call(body, outs, scalars, arrays, scratch=(), cost=2_000_000):
    return pl.pallas_call(
        body,
        out_shape=[
            out if isinstance(out, jax.ShapeDtypeStruct) else jax.ShapeDtypeStruct(out, F32)
            for out in outs
        ],
        in_specs=[IN_SMEM] * len(scalars) + [IN_VMEM] * len(arrays),
        out_specs=[IN_VMEM] * len(outs),
        scratch_shapes=list(scratch),
        compiler_params=pltpu.CompilerParams(vmem_limit_bytes=VMEM_GRANT),
        cost_estimate=pl.CostEstimate(flops=cost, bytes_accessed=cost, transcendentals=0),
    )(*scalars, *arrays)


def exchanged(value, axis):
    peers = lax.axis_size(axis)
    return [value] + [
        lax.ppermute(value, axis, [(i, i ^ mask) for i in range(peers)]) for mask in range(1, peers)
    ]


def swapped(value, axis):
    return lax.all_to_all(value, axis, split_axis=0, concat_axis=0, tiled=True)


def across_outer(value, axis):
    peers = lax.axis_size(axis)
    up = [(i, i + 1) for i in range(1, peers - 1, 2)]
    return lax.ppermute(value, axis, up + [(j, i) for i, j in up])


def across_inner(value, axis):
    return lax.ppermute(value, axis, [(i, i ^ 1) for i in range(lax.axis_size(axis))])


def each(count, body):
    if count <= 16:
        for step in range(count):
            body(step)
    else:
        lax.fori_loop(0, count, lambda step, carry: (body(step), carry)[1], 0)


def lanes(block, length):
    start = block * length
    return pl.ds(start if isinstance(block, int) else pl.multiple_of(start, length), length)


def padded(value, rows):
    if value.shape[0] == rows:
        return value
    return jnp.concatenate([value, jnp.zeros((rows - value.shape[0], value.shape[1]), F32)], axis=0)


def in_parts(value):
    pieces = []
    for _ in range(PARTS):
        piece = value.astype(jnp.bfloat16)
        pieces.append(piece)
        value = value - piece.astype(F32)
    return jnp.concatenate(pieces, axis=0)


def fill(field, base, value, length):
    split = in_parts(value)
    for block in range(value.shape[1] // length):
        field[base + block, : split.shape[0], :] = split[:, block * length : (block + 1) * length]


def split(block, blocks):
    if blocks & (blocks - 1):
        return lax.div(block, blocks), lax.rem(block, blocks)
    bits = blocks.bit_length() - 1
    return lax.shift_right_logical(block, bits), lax.bitwise_and(block, blocks - 1)


def parity_of(index):
    return lax.bitwise_and(split(index[0, 0], index.shape[1])[0], 1)


def half(parity, vertices, width, length):
    return pl.ds(pl.multiple_of(parity * (vertices - width), length), width)


def fill_extended(field, parity, outer, own, inner, length):
    margin, blocks = outer.shape[1] // length, own.shape[1] // length
    fill(field, parity * (margin + blocks), outer, length)
    fill(field, margin, own, length)
    fill(field, (1 - parity) * (margin + blocks), inner, length)


def neighbours(index, weight, field, block):
    shift = index.shape[1] // 2 - index[0, 0]
    total = None
    for k in range(index.shape[0]):
        term = lax.dot_general(
            field[index[k, block] + shift],
            weight[block, k],
            (((1,), (1,)), ((), ())),
            preferred_element_type=F32,
        )
        total = term if total is None else total + term
    return total


def folded(total, rows):
    return total[:rows] + total[rows : 2 * rows] + total[2 * rows : PARTS * rows]


def solved(matrix, size):
    row_id = lax.broadcasted_iota(jnp.int32, matrix.shape, 0)
    step = 8 if size % 8 == 0 else 1
    for base in range(0, size, step):
        ids = range(step)
        columns = [
            jnp.broadcast_to(matrix[:, base + j : base + j + 1], matrix.shape) for j in ids
        ]
        block = [[columns[j][base + i : base + i + 1] for j in ids] for i in ids]
        lines = [matrix[base + i : base + i + 1] for i in ids]
        for i in ids:
            scale = 1.0 / block[i][i]
            lines[i] = lines[i] * scale
            for j in range(i + 1, step):
                block[i][j] = block[i][j] * scale
            for other in ids:
                if other == i:
                    continue
                factor = block[other][i]
                lines[other] = lines[other] - factor * lines[i]
                for j in range(i + 1, step):
                    block[other][j] = block[other][j] - factor * block[i][j]
        for j in ids:
            matrix = matrix - columns[j] * lines[j]
        for j in ids:
            matrix = jnp.where(row_id == base + j, lines[j], matrix)
    return matrix


def local(states, adj_weight, adj_index, partner):
    local_cols, vertices = states.shape
    blocks, entries, length, _ = adj_weight.shape
    row_devices, col_devices = lax.axis_size("rows"), lax.axis_size("cols")
    total_cols = local_cols * col_devices
    margin = blocks // 2
    width = margin * length
    rows = -(-local_cols // 16) * 16
    packed_rows = total_cols // 2
    field_shape = (2 * blocks, PARTS * rows, length)
    field = pltpu.VMEM(field_shape, jnp.bfloat16)
    full, edge, line = (rows, vertices), (rows, width), (1, vertices)
    slots = (2 * row_devices, rows, length)

    def halves(parity):
        return (
            half(parity, vertices, width, length),
            half(1 - parity, vertices, width, length),
        )

    def place(out, mate, value):
        owner, position = split(mate, blocks)
        side = lax.bitwise_and(owner, 1)
        beside = owner + 2 * side - 1
        high = lax.select(position >= margin, 1, 0)
        wanted = (high == side) & (beside >= 0) & (beside < row_devices)
        out[2 * owner] = value
        out[lax.select(wanted, 2 * beside + 1, 2 * owner)] = value

    def ones_body(ones):
        ones[...] = jnp.ones(ones.shape, ones.dtype)

    def degree_body(ones, weight, index, mates, degree):
        def one(block):
            total = None
            for k in range(weight.shape[1]):
                term = lax.dot_general(
                    ones[...],
                    weight[block, k],
                    (((1,), (1,)), ((), ())),
                    preferred_element_type=F32,
                )
                total = term if total is None else total + term
            degree[:, lanes(block, length)] = total[:1]

        each(blocks, one)

    def image_body(index, mates, weight, degree, outer_states, inner_states, states, *refs):
        image, sent, scaled, outer, inner, degrees, spread = refs
        parity = parity_of(index)
        at_own_outer, at_own_inner = halves(parity)
        fill_extended(
            spread,
            parity,
            padded(outer_states[:, at_own_inner], rows),
            padded(states[...], rows),
            padded(inner_states[:, at_own_outer], rows),
            length,
        )

        def one(block):
            value = folded(neighbours(index, weight, spread, block), rows)
            at = lanes(block, length)
            image[:, at] = value
            scaled[:, at] = value / degree[:, at]

        each(blocks, one)
        for block in range(blocks):
            degrees[split(mates[block], blocks)[0]] = degree[:, lanes(block, length)]
        sent[...] = image[:local_cols, :]
        inner[...] = scaled[:, at_own_inner]
        outer[:, :width] = scaled[:, at_own_outer]
        lane = lax.broadcasted_iota(jnp.int32, (rows, length), 1)
        listed = jnp.zeros((rows, length), jnp.int32)
        for block in range(blocks):
            listed = jnp.where(lane == block, mates[block], listed)
        outer[:, width:] = listed.astype(F32)

    def products_body(*refs):
        peers, (image, degree, degrees, shared, wide, flat) = (
            refs[:col_devices],
            refs[col_devices:],
        )
        everyone = jnp.concatenate([peer[...] for peer in peers], axis=0)
        other = jnp.concatenate([everyone * degree[...], image[...]], axis=0)
        wide[...] = jnp.zeros(wide.shape, F32)
        wide[:, : total_cols + rows] = lax.dot_general(
            everyone,
            other,
            (((1,), (1,)), ((), ())),
            precision=EXACT,
            preferred_element_type=F32,
        )
        packed = wide[:packed_rows, :] + pltpu.roll(wide[packed_rows:, :], length // 2, 1)
        for row in range(packed_rows):
            flat[:, lanes(row, length)] = packed[row : row + 1]
        value = flat[...]
        for device in range(row_devices):
            shared[device, :, : packed_rows * length] = value
            shared[device, :, packed_rows * length :] = degrees[device]

    def solve_body(shared, ritz, tall):
        total = shared[0, :, : packed_rows * length]
        for device in range(1, row_devices):
            total = total + shared[device, :, : packed_rows * length]
        for row in range(packed_rows):
            tall[row : row + 1, :] = total[:, row * length : (row + 1) * length]
        total = tall[...]
        total = jnp.concatenate([total, pltpu.roll(total, length // 2, 1)], axis=0)
        ritz[...] = jnp.transpose(solved(total, total_cols))[total_cols : total_cols + rows]

    def remain_body(index, mates, weight, outer, inner, shared, ritz, *refs):
        peers, refs = refs[:col_devices], refs[col_devices:]
        images, refs = refs[:col_devices], refs[col_devices:]
        own_image, scaled, degree, *refs = refs
        out, remain, residual, presmooth, pair_degree, beside, spread_field = refs
        parity = parity_of(index)
        fill_extended(spread_field, parity, outer[:, :width], scaled[...], inner[...], length)

        def offset(block):
            at = lanes(block, length)
            value = folded(neighbours(index, weight, spread_field, block), rows)
            remain[:, at] = KEEP * own_image[:, at] + DAMPING * value

        each(blocks, offset)
        everyone = jnp.concatenate([peer[...] for peer in peers], axis=0)
        spread = jnp.concatenate([image[...] for image in images], axis=0)
        mixed = jnp.dot(ritz[...], everyone, precision=EXACT, preferred_element_type=F32)
        mixed_image = jnp.dot(ritz[...], spread, precision=EXACT, preferred_element_type=F32)
        weighted = degree[...] * mixed
        residual[...] = weighted - own_image[...]
        presmooth[...] = DAMPING * (mixed - scaled[...])
        remain[...] = KEEP * weighted + DAMPING * mixed_image - remain[...]

        def one(block):
            at = lanes(block, length)
            place(out, mates[block], remain[:, at])
            owner, _ = split(mates[block], blocks)
            pair_degree[:, at] = degree[:, at] + shared[owner, :, packed_rows * length :]

        each(blocks, one)
        at_outer, _ = halves(parity)
        beside[:, :width] = remain[:, at_outer]
        beside[:, width:] = jnp.zeros((rows, length), F32)
        shared_degree = pair_degree[:, at_outer]
        for block in range(margin):
            beside[block : block + 1, width:] = shared_degree[:, block * length : (block + 1) * length]

    def masks_body(index, mates, outer_mates, masks):
        parity = parity_of(index)
        source = lax.broadcasted_iota(jnp.int32, (row_devices, length), 0)
        for block in range(blocks + margin):
            if block < blocks:
                mate = mates[block]
            else:
                mate = outer_mates[(1 - parity) * margin + block - blocks]
            here = source == split(mate, blocks)[0]
            masks[block * row_devices : (block + 1) * row_devices, :] = jnp.where(here, 1.0, 0.0)
        base = (blocks + margin) * row_devices
        masks[base : base + 8, :] = jnp.full((8, length), parity, F32)
        base += 8
        place_id = lax.broadcasted_iota(jnp.int32, (margin, length), 0)
        first = (1 - parity) * (margin + blocks) - margin + index[0, 0]
        for pair in range(blocks * (entries - 1)):
            block, k = pair // (entries - 1), 1 + pair % (entries - 1)
            here = place_id == index[k, block] - first
            masks[base + pair * margin : base + (pair + 1) * margin, :] = jnp.where(here, 1.0, 0.0)

    def chosen(masks, arrived, block, slot):
        value = arrived[slot]
        for device in range(1, row_devices):
            row = block * row_devices + device
            here = jnp.broadcast_to(masks[row : row + 1, :], (rows, length)) > 0.5
            value = jnp.where(here, arrived[2 * device + slot], value)
        return value

    def inner_terms(masks, weight, inner, block):
        base = (blocks + margin) * row_devices + 8
        total = None
        for k in range(1, entries):
            start = base + (block * (entries - 1) + k - 1) * margin
            value = jnp.zeros((rows, length), F32)
            for j in range(margin):
                row = masks[start + j : start + j + 1, :]
                here = jnp.broadcast_to(row, (rows, length)) > 0.5
                value = jnp.where(here, inner[:, lanes(j, length)], value)
            term = lax.dot_general(
                in_parts(value),
                weight[block, k],
                (((1,), (1,)), ((), ())),
                preferred_element_type=F32,
            )
            total = term if total is None else total + term
        return folded(total, rows)

    def inner_half(masks, value):
        row = (blocks + margin) * row_devices
        odd = jnp.broadcast_to(masks[row : row + 1, :1], (rows, width)) > 0.5
        return jnp.where(odd, value[:, :width], value[:, vertices - width :])

    def coarse_body(masks, arrived, beside, remain, pair_degree, coarse, fix, further, inner):
        def one(block):
            at = lanes(block, length)
            value = remain[:, at] + chosen(masks, arrived, block, 0)
            coarse[:, at] = value
            fix[:, at] = DAMPING * value / pair_degree[:, at]

        def other(block):
            at = lanes(block, length)
            value = beside[:, at] + chosen(masks, arrived, blocks + block, 1)
            further[:rows, at] = DAMPING * value / beside[block : block + 1, width:]
            further[rows:, at] = value

        for block in range(blocks):
            one(block)
        for block in range(margin):
            other(block)
        inner[...] = inner_half(masks, fix[...])

    def product_body(
        index, mates, weight, further, inner, fix, degree, presmooth, pair_degree, *refs
    ):
        out, product, outer, spread = refs
        fill_extended(spread, parity_of(index), further[:rows, :], fix[...], inner[...], length)

        def one(block):
            at = lanes(block, length)
            value = degree[:, at] * fix[:, at] - folded(neighbours(index, weight, spread, block), rows)
            product[:, at] = value

        each(blocks, one)
        each(blocks, lambda block: place(out, mates[block], product[:, lanes(block, length)]))
        at_outer, _ = halves(parity_of(index))
        step = DAMPING * product[:, at_outer] / pair_degree[:, at_outer]
        outer[...] = presmooth[:, at_outer] - step

    def fix_body(masks, arrived, partial, beside, further, *refs):
        product, coarse, fix, pair_degree, presmooth, second, outer, inner = refs

        def one(block):
            at = lanes(block, length)
            image = product[:, at] + chosen(masks, arrived, block, 0)
            step = DAMPING * (coarse[:, at] - image) / pair_degree[:, at]
            second[:, at] = presmooth[:, at] + (fix[:, at] + step)

        def other(block):
            at = lanes(block, length)
            image = further[rows:, at] - chosen(masks, arrived, blocks + block, 1)
            step = DAMPING * image / beside[block : block + 1, width:]
            outer[:, at] = partial[:, at] + (further[:rows, at] + step)

        for block in range(blocks):
            one(block)
        for block in range(margin):
            other(block)
        inner[...] = inner_half(masks, second[...])

    def diagonal():
        lane = lax.broadcasted_iota(jnp.int32, (rows, length), 1)
        return lane == lax.broadcasted_iota(jnp.int32, (rows, length), 0)

    def smooth_early_body(index, weight, outer, second, residual, degree, early, spread):
        nothing = jnp.zeros((rows, width), F32)
        fill_extended(spread, parity_of(index), outer[...], second[...], nothing, length)

        def one(block):
            at = lanes(block, length)
            value, here = second[:, at], degree[:, at]
            image = here * value - folded(neighbours(index, weight, spread, block), rows)
            early[:, at] = value + DAMPING * (residual[:, at] - image) / here

        each(blocks, one)

    def smooth_body(masks, weight, inner, early, degree, smooth, squares):
        for block in range(blocks):
            at = lanes(block, length)
            step = DAMPING * inner_terms(masks, weight, inner, block) / degree[:, at]
            smooth[:, at] = early[:, at] + step
        value = smooth[...]
        total = jnp.broadcast_to(jnp.sum(value * value, axis=1, keepdims=True), (rows, length))
        packed = jnp.sum(jnp.where(diagonal(), total, 0.0), axis=0, keepdims=True)
        for device in range(row_devices):
            squares[device] = packed

    def scale_body(squares, smooth, correction):
        total = squares[0]
        for device in range(1, row_devices):
            total = total + squares[device]
        total = jnp.where(diagonal(), jnp.broadcast_to(total, (rows, length)), 0.0)
        total = jnp.sum(total, axis=1, keepdims=True)
        norm = jnp.sqrt(total[:local_cols] / (vertices * row_devices) + EPSILON)
        correction[...] = smooth[:local_cols, :] / norm

    adj_index = adj_index.T
    outer = across_outer(states, "rows")
    inner = across_inner(states, "rows")
    peers = exchanged(states, "cols")
    ones_shape = jax.ShapeDtypeStruct((16, length), jnp.bfloat16)
    (ones,) = kernel_call(ones_body, [ones_shape], [], [], cost=20_000_000_000)
    (degree,) = kernel_call(degree_body, [line], [], [ones, adj_weight, adj_index, partner])
    image, sent, scaled, outer, inner, degrees = kernel_call(
        image_body,
        [
            full,
            (local_cols, vertices),
            full,
            (rows, width + length),
            edge,
            (row_devices, 1, length),
        ],
        [adj_index, partner],
        [adj_weight, degree, outer, inner, states],
        [field],
    )
    (shared,) = kernel_call(
        products_body,
        [(row_devices, 1, (packed_rows + 1) * length)],
        [],
        [*peers, image, degree, degrees],
        [pltpu.VMEM((total_cols, length), F32), pltpu.VMEM((1, packed_rows * length), F32)],
    )
    shared = swapped(shared, "rows")
    outer = across_outer(outer, "rows")
    inner = across_inner(inner, "rows")
    images = exchanged(sent, "cols")
    outer_mates = outer[0, width : width + blocks].astype(jnp.int32)
    (ritz,) = kernel_call(
        solve_body, [(rows, total_cols)], [], [shared], [pltpu.VMEM((packed_rows, length), F32)]
    )
    out, remain, residual, presmooth, pair_degree, beside = kernel_call(
        remain_body,
        [slots, full, full, full, line, (rows, width + length)],
        [adj_index, partner],
        [adj_weight, outer, inner, shared, ritz, *peers, *images, image, scaled, degree],
        [field],
    )
    arrived = swapped(out, "rows")
    beside = across_outer(beside, "rows")
    (masks,) = kernel_call(
        masks_body,
        [((blocks + margin) * row_devices + 8 + blocks * (entries - 1) * margin, length)],
        [adj_index, partner, outer_mates],
        [],
    )
    coarse, fix, further, inner = kernel_call(
        coarse_body,
        [full, full, (2 * rows, width), edge],
        [],
        [masks, arrived, beside, remain, pair_degree],
    )
    inner = across_inner(inner, "rows")
    out, product, outer = kernel_call(
        product_body,
        [slots, full, edge],
        [adj_index, partner],
        [adj_weight, further, inner, fix, degree, presmooth, pair_degree],
        [field],
    )
    arrived = swapped(out, "rows")
    outer = across_outer(outer, "rows")
    second, outer, inner = kernel_call(
        fix_body,
        [full, edge, edge],
        [],
        [masks, arrived, outer, beside, further, product, coarse, fix, pair_degree, presmooth],
    )
    inner = across_inner(inner, "rows")
    (early,) = kernel_call(
        smooth_early_body,
        [full],
        [adj_index],
        [adj_weight, outer, second, residual, degree],
        [field],
    )
    smooth, squares = kernel_call(
        smooth_body, [full, (row_devices, 1, length)], [], [masks, adj_weight, inner, early, degree]
    )
    squares = swapped(squares, "rows")
    (correction,) = kernel_call(scale_body, [states.shape], [], [squares, smooth])
    return correction


def solution(mesh):
    return jax.shard_map(
        local,
        mesh=mesh,
        in_specs=(P("cols", "rows"), P("rows", None, None, None), P("rows", None), P("rows")),
        out_specs=P("cols", "rows"),
        check_vma=False,
    )
```
